128 devices in a mesh: section: 2 (over x_hi), tp: 2 (over core), dp: 32 (over z, y, x_lo).
Axes of the slice: x: 4 (x_hi: 2, x_lo: 2; x = x_hi * 2 + x_lo), y: 4, z: 4, core: 2. Of those that a mesh axis runs over, the one named last changes fastest.
Arguments:
- tokens_in: bfloat16 [32, 512, 4096], P('dp', None, 'tp'), may hold values from -6 to 6
- patches: bfloat16 [32, 256, 32], P('dp'), may hold values from -6 to 6
- segment_ids: int32 [32, 512], P('dp'), may hold values from 0 to 3, never falling along the last dimension, each value on 1 to 256 neighbouring positions
- img_start: int32 [32], P('dp'), may hold values from 0 to 256
- img_count: int32 [32], P('dp'), may hold values from 0 to 1
- norm_gain: float32 [2, 4096], P('section'), may hold values from 0.1 to 1.9
- w_qkv: bfloat16 [2, 4096, 16, 3, 128], P('section', 'dp', 'tp'), may hold values from -2 to 2
- w_out: bfloat16 [2, 2048, 4096], P('section', 'dp', 'tp'), may hold values from -0.125 to 0.125
- w_down1: bfloat16 [32, 512], replicated, may hold values from -1 to 1
- w_down2: bfloat16 [512, 4096], P(None, 'tp'), may hold values from -0.25 to 0.25
- w_up1: bfloat16 [4096, 512], P('tp'), may hold values from -0.09375 to 0.09375
- w_up2: bfloat16 [512, 32], P(None, 'section'), may hold values from -0.25 to 0.25
- cotangent: bfloat16 [32, 256, 32], P('dp', None, 'section'), may hold values from -6 to 6
Outputs:
- hidden_states: bfloat16 [2, 32, 512, 4096], P('section', 'dp', None, 'tp')
- image_pred: bfloat16 [32, 256, 32], P('dp', None, 'section')
- grad_up: float32 [512, 32], P(None, 'section')
The draws below stay inside these ranges and needn't reach their ends.
Inputs may be any that keep to these rules, and one draw needn't show every extreme that they name: `segment_ids`: document of each position; never falls along a micro-batch, each document covers 1 to 256 positions.
All inputs are finite; a program needn't handle non-finite values.
Results may differ from the reference program's by a relative error of at most 0.019.
Values may be sent and summed in bfloat16 or wider, within the bound.
A program may use at most 128 MiB of HBM per device.

```python
import math
import jax
import jax.numpy as jnp
import numpy as np
from jax import lax

D = 4096
HEADS = 16
HD = 128
UC = 512
PIX = 32
IMG_TOK = 256
ROWS = 512
DOCS = 4
DOC_MOST = 256
LAYERS = 2
MBS = 32


def draw_w_qkv(key, part):
    first = jax.random.fold_in(jax.random.fold_in(key, 7), 0)
    base = jax.random.truncated_normal(first, -6.0, 6.0, (LAYERS, D, HEADS, 3, HD), jnp.float32) / math.sqrt(D)
    return jnp.clip(base, -2.0, 2.0).astype(jnp.bfloat16)


def touch_ends(drawn, own_key, low, largest):
    extent = drawn.shape
    index_at = [jax.random.randint(jax.random.fold_in(own_key, axis), (), 0, extent[axis]) for axis in range(len(extent))]
    drawn = drawn.at[tuple(index_at)].set(low)
    longest = extent.index(max(extent))
    index_at[longest] = (index_at[longest] + 1) % extent[longest]
    return drawn.at[tuple(index_at)].set(largest)


def steps_of(rng, shape, shards, smallest, high):
    loudness, own = 1.0, jax.random.fold_in(rng, 6)
    for dim, shards_of in shards:
        steps = jnp.exp(jax.random.uniform(jax.random.fold_in(own, dim), (shards_of,), jnp.float32, smallest / len(shards), high / len(shards)))
        loudness = loudness * jnp.repeat(steps, shape[dim] // shards_of).reshape([-1 if axis == dim else 1 for axis in range(len(shape))])
    return loudness


def length_profile(number_of, total, most, lean):
    loads = [(1 << 20) // math.isqrt(rank ** lean) + 1 for rank in range(2, number_of + 1)]
    rest, holding = total - most - (number_of - 1), [1] * (number_of - 1)
    while rest > 0:
        free = [i for i in range(number_of - 1) if holding[i] < most]
        mass, budget = sum([loads[i] for i in free]), rest
        for i in free:
            extra = min(most - holding[i], max(1, budget * loads[i] // mass), rest)
            holding[i] = holding[i] + extra
            rest = rest - extra
    return np.array([most] + holding)


def ragged(key, count, total, limit, slope):
    if count == 2:
        one = jax.random.randint(key, (), max(1, total - limit), min(limit, total - 1) + 1)
        return jnp.stack([one, total - one])
    sizes = jnp.asarray(length_profile(count, total, limit, slope), jnp.int32)
    twos = (count - 1) // 2
    source_of, sink = sizes[1:1 + 2 * twos:2], sizes[2:2 + 2 * twos:2]
    margin = jnp.minimum(source_of - 1, limit - sink)
    shifted = jax.random.randint(jax.random.fold_in(key, 1), (twos,), 0, 1 << 20) % (margin + 1)
    sizes = sizes.at[1:1 + 2 * twos:2].set(source_of - shifted).at[2:2 + 2 * twos:2].set(sink + shifted)
    return sizes[jax.random.permutation(jax.random.fold_in(key, 2), count)]


def noise(key, dims, width, limit, cuts=(), kind=jnp.bfloat16):
    entries = width * jax.random.normal(key, dims, jnp.float32)
    if cuts:
        entries = entries * steps_of(key, dims, cuts, -0.22, 0.18)
    return jnp.clip(entries, -limit, limit).astype(kind)


def setup_inputs(seed: int = 0) -> dict:
    key_of = jax.random.split(jax.random.key(seed), 14)
    tokens_in = noise(key_of[0], (MBS, ROWS, D), 1.0, 6.0, ((0, 32), (2, 2)))
    patches = noise(key_of[1], (MBS, IMG_TOK, PIX), 1.0, 6.0, ((0, 32),))
    segment_ids = jax.vmap(lambda own: jnp.searchsorted(jnp.cumsum(ragged(own, DOCS, ROWS, DOC_MOST, 0)), jnp.arange(ROWS), side="right"))(jax.random.split(key_of[2], MBS)).reshape((MBS, ROWS)).astype(jnp.int32)
    img_start = touch_ends(jax.random.randint(key_of[3], (MBS,), 0, ROWS - IMG_TOK + 1), jax.random.fold_in(key_of[3], 1), 0, ROWS - IMG_TOK).astype(jnp.int32)
    img_count = touch_ends(jax.random.randint(key_of[4], (MBS,), 0, 2), jax.random.fold_in(key_of[4], 1), 0, 1).astype(jnp.int32)
    norm_gain = jnp.clip(1.0 + 0.18 * jax.random.normal(key_of[5], (LAYERS, D), jnp.float32), 0.1, 1.9)
    w_qkv = draw_w_qkv(jax.random.fold_in(key_of[13], 71), 0)
    w_out = noise(key_of[7], (LAYERS, HEADS * HD, D), (HEADS * HD) ** -0.5, 0.125, ((0, 2), (1, 32), (2, 2)))
    w_down1 = noise(key_of[8], (PIX, UC), PIX ** -0.5, 1.0)
    w_down2 = noise(key_of[9], (UC, D), UC ** -0.5, 0.25, ((1, 2),))
    w_up1 = noise(key_of[10], (D, UC), D ** -0.5, 0.09375, ((0, 2),))
    w_up2 = noise(key_of[11], (UC, PIX), UC ** -0.5, 0.25, ((1, 2),))
    cotangent = noise(key_of[12], (MBS, IMG_TOK, PIX), 1.0, 6.0, ((0, 32), (2, 2)))
    return {"tokens_in": tokens_in, "patches": patches, "segment_ids": segment_ids, "img_start": img_start, "img_count": img_count, "norm_gain": norm_gain, "w_qkv": w_qkv, "w_out": w_out, "w_down1": w_down1, "w_down2": w_down2, "w_up1": w_up1, "w_up2": w_up2, "cotangent": cotangent}


EPSILON = 1e-05

def unet_down(patches, w_down1, w_down2):
    inner = jnp.einsum('mkp,pc->mkc', patches.astype(jnp.float32), w_down1.astype(jnp.float32))
    skipped = jax.nn.silu(inner).astype(jnp.bfloat16)
    tokens = jnp.einsum('mkc,cd->mkd', skipped.astype(jnp.float32), w_down2.astype(jnp.float32))
    return (skipped, tokens.astype(jnp.bfloat16))

def place_images(tokens_in, image_tokens, img_start, img_count):

    def single(rows, image, start, count):
        placed = lax.dynamic_update_slice_in_dim(rows, image, start.astype(jnp.int32), 0)
        return jnp.where(count > 0, placed, rows)
    return jax.vmap(single)(tokens_in, image_tokens, img_start, img_count)

def allowed_pairs(segment, start, count, rows, img_tok):
    position = jnp.arange(rows, dtype=jnp.int32)
    in_image = (count > 0) & (position >= start) & (position < start + img_tok)
    same = segment[:, None] == segment[None, :]
    causal = position[None, :] <= position[:, None]
    return same & (causal | in_image[:, None] & in_image[None, :])

def rms_normed(full, gain):
    values = full.astype(jnp.float32)
    mean_sq = lax.optimization_barrier(jnp.mean(values * values, axis=-1, keepdims=True))
    return (values * lax.rsqrt(mean_sq + EPSILON) * gain).astype(jnp.bfloat16)

def attend(normed, weights_qkv, allowed):
    heads, hdim = (weights_qkv.shape[1], weights_qkv.shape[3])
    proj = jnp.einsum('rd,dhtk->rhtk', normed.astype(jnp.float32), weights_qkv.astype(jnp.float32)).astype(jnp.bfloat16)
    query, keys, values = (proj[:, :, 0], proj[:, :, 1], proj[:, :, 2])
    scores = jnp.einsum('qhk,shk->hqs', query.astype(jnp.float32), keys.astype(jnp.float32)) / math.sqrt(hdim)
    scores = jnp.where(allowed[None], scores, -1e+30)
    probs = jnp.exp(scores - lax.optimization_barrier(jnp.max(scores, axis=-1, keepdims=True)))
    probs = (probs / lax.optimization_barrier(jnp.sum(probs, axis=-1, keepdims=True))).astype(jnp.bfloat16)
    mixed = jnp.einsum('hqs,shk->qhk', probs.astype(jnp.float32), values.astype(jnp.float32)).astype(jnp.bfloat16)
    return mixed.reshape(mixed.shape[0], heads * hdim)

def reference(tokens_in, patches, segment_ids, img_start, img_count, norm_gain, w_qkv, w_out, w_down1, w_down2, w_up1, w_up2, cotangent):
    skipped, image_tokens = unet_down(patches, w_down1, w_down2)
    current = place_images(tokens_in, image_tokens, img_start, img_count)
    masks = jax.vmap(lambda seg, st, ct: allowed_pairs(seg, st, ct, ROWS, IMG_TOK))(segment_ids, img_start, img_count)
    states = []
    for layer in range(LAYERS):
        normed = rms_normed(current, norm_gain[layer])
        weights_now = w_qkv[layer]
        mixed = lax.map(lambda pair: attend(pair[0], weights_now, pair[1]), (normed, masks))
        added = jnp.einsum('mre,ed->mrd', mixed.astype(jnp.float32), w_out[layer].astype(jnp.float32))
        current = (current.astype(jnp.float32) + added).astype(jnp.bfloat16)
        states.append(current)
    hidden_states = jnp.stack(states)
    final_rows = jax.vmap(lambda rows, st: lax.dynamic_slice_in_dim(rows, st.astype(jnp.int32), IMG_TOK, 0))(current, img_start)
    summed = jnp.einsum('mkd,dc->mkc', final_rows.astype(jnp.float32), w_up1.astype(jnp.float32))
    upper = jax.nn.silu(summed + skipped.astype(jnp.float32)).astype(jnp.bfloat16)
    present = (img_count > 0)[:, None, None]
    projected = jnp.einsum('mkc,cp->mkp', upper.astype(jnp.float32), w_up2.astype(jnp.float32))
    image_pred = jnp.where(present, projected, 0.0).astype(jnp.bfloat16)
    weighted = jnp.where(present, cotangent.astype(jnp.float32), 0.0)
    grad_up = jnp.einsum('mkc,mkp->cp', upper.astype(jnp.float32), weighted)
    return (hidden_states, image_pred, grad_up)
```

```python
import functools
import math

import jax
import jax.numpy as jnp
from jax import lax
from jax.experimental import pallas as pl
from jax.experimental.pallas import tpu as pltpu
from jax.sharding import PartitionSpec as P

EPSILON = 1e-05
MESH = pl.DeviceIdType.MESH
ANY = pl.BlockSpec(memory_space=pl.ANY)
VM = pl.BlockSpec(memory_space=pltpu.VMEM)
RING = 4


class Place:
    def __init__(self):
        self.s = lax.axis_index("section")
        self.c = lax.axis_index("tp")
        d = lax.axis_index("dp")
        self.k = lax.rem(d, 2)
        self.y = lax.rem(lax.div(d, 2), RING)
        self.z = lax.div(d, 2 * RING)
        self.x = 2 * self.s + self.k

    def at(self, dx=0, dy=0, dz=0, sibling=False):
        x = lax.rem(self.x + dx, RING)
        y = lax.rem(self.y + dy, RING)
        z = lax.rem(self.z + dz, RING)
        return {
            "section": lax.div(x, 2),
            "tp": 1 - self.c if sibling else self.c,
            "dp": z * 8 + y * 2 + lax.rem(x, 2),
        }


def greet(peers):
    barrier = pltpu.get_barrier_semaphore()
    for peer in peers:
        pl.semaphore_signal(barrier, inc=1, device_id=peer, device_id_type=MESH)
    pl.semaphore_wait(barrier, len(peers))


def remote(src, dst, send, recv, peer):
    return pltpu.make_async_remote_copy(
        src_ref=src, dst_ref=dst, send_sem=send, recv_sem=recv, device_id=peer, device_id_type=MESH
    )


def gather_kernel(
    wq, wo, xin, gain, meta, q_all, o_all, x_all, g_all, m_all, s0, r0, s1, r1, s2, r2, sx, rx, loc
):
    me = Place()
    s, c, k, x, y, z = me.s, me.c, me.k, me.x, me.y, me.z
    greet([me.at(dx=j) for j in (1, 2, 3)] + [me.at(dy=1), me.at(dy=3), me.at(dz=1), me.at(dz=3)]
          + [me.at(sibling=True)])
    pending = []
    for a, (src, dst) in enumerate(((wq, q_all), (wo, o_all))):
        for j in (1, 2, 3):
            peer_x = lax.rem(x + j, RING)
            cp = remote(src.at[peer_x], dst.at[s, z, y, k], s0.at[a, j], r0.at[a, x], me.at(dx=j))
            cp.start()
            pending.append(cp)
        pltpu.make_async_copy(src.at[x], dst.at[s, z, y, k], r0.at[a, x]).start()
    width = xin.shape[1]
    half = xin.shape[0] // 2
    cols = pl.ds(pl.multiple_of(c * width, width), width)
    x_loc = pltpu.make_async_copy(xin, x_all.at[k, :, cols], loc.at[0])
    g_loc = pltpu.make_async_copy(gain, g_all.at[s], loc.at[1])
    m_loc = pltpu.make_async_copy(meta, m_all.at[k], loc.at[2])
    for cp in (x_loc, g_loc, m_loc):
        cp.start()
    low, high = pl.ds(0, half), pl.ds(half, half)
    up = remote(xin.at[low], x_all.at[k, low, cols], sx.at[0], rx.at[0], me.at(dx=1))
    down = remote(xin.at[high], x_all.at[k, high, cols], sx.at[1], rx.at[1], me.at(dx=3))
    side = remote(xin, x_all.at[k, :, cols], sx.at[2], rx.at[2], me.at(sibling=True))
    g_cp = remote(gain, g_all.at[s], sx.at[3], rx.at[3], me.at(dx=2))
    m_cp = remote(meta, m_all.at[k], sx.at[4], rx.at[4], me.at(dx=1))
    for cp in (up, down, side, g_cp, m_cp):
        cp.start()

    def spot(ref, layer, kk, zz, yy, rows=None):
        view = ref.at[layer, zz, yy, kk]
        return view if rows is None else view.at[rows]

    items = [(layer, kk) for layer in (0, 1) for kk in (0, 1)]
    ring1 = {}
    for i, (layer, kk) in enumerate(items):
        for a, ref in enumerate((q_all, o_all)):
            own = spot(ref, layer, kk, z, y)
            pltpu.make_async_copy(own, own, r0.at[a, i]).wait()
            for direction in (0, 1):
                step = 1 if direction == 0 else 3
                peer = me.at(dy=step) if kk == 0 else me.at(dz=step)
                cp = remote(own, own, s1.at[a, i, direction], r1.at[a, i, direction], peer)
                cp.start()
                ring1[a, i, direction] = cp
    for i, (layer, kk) in enumerate(items):
        for a, ref in enumerate((q_all, o_all)):
            rows = ref.shape[4]
            for direction in (0, 1):
                step = 1 if direction == 0 else 3
                ring1[a, i, direction].wait_recv()
                zz = z if kk == 0 else lax.rem(z + 4 - step, RING)
                yy = lax.rem(y + 4 - step, RING) if kk == 0 else y
                part = spot(ref, layer, kk, zz, yy, pl.ds(direction * rows // 2, rows // 2))
                peer = me.at(dy=step) if kk == 0 else me.at(dz=step)
                cp = remote(part, part, s1.at[a, i, 2 + direction], r1.at[a, i, 2 + direction], peer)
                cp.start()
                ring1[a, i, 2 + direction] = cp
    ring2 = {}

    def band(ref, layer, kk, zz, yy, part=None):
        if part is None:
            return ref.at[layer, zz, :, kk] if kk == 0 else ref.at[layer, :, yy, kk]
        piece = pl.ds(2 * part, 2)
        return ref.at[layer, zz, piece, kk] if kk == 0 else ref.at[layer, piece, yy, kk]

    for i, (layer, kk) in enumerate(items):
        for a, ref in enumerate((q_all, o_all)):
            for direction in (0, 1):
                ring1[a, i, 2 + direction].wait_recv()
            own = band(ref, layer, kk, z, y)
            for direction in (0, 1):
                step = 1 if direction == 0 else 3
                peer = me.at(dz=step) if kk == 0 else me.at(dy=step)
                cp = remote(own, own, s2.at[a, i, direction], r2.at[a, i, direction], peer)
                cp.start()
                ring2[a, i, direction] = cp
    other = 1 - k
    up.wait_recv()
    side_low = remote(x_all.at[other, low, cols], x_all.at[other, low, cols], sx.at[5], rx.at[5],
                      me.at(sibling=True))
    side_low.start()
    down.wait_recv()
    side_high = remote(x_all.at[other, high, cols], x_all.at[other, high, cols], sx.at[6], rx.at[6],
                       me.at(sibling=True))
    side_high.start()
    for i, (layer, kk) in enumerate(items):
        for a, ref in enumerate((q_all, o_all)):
            for direction in (0, 1):
                step = 1 if direction == 0 else 3
                ring2[a, i, direction].wait_recv()
                zz = lax.rem(z + 4 - step, RING) if kk == 0 else z
                yy = y if kk == 0 else lax.rem(y + 4 - step, RING)
                part = band(ref, layer, kk, zz, yy, direction)
                peer = me.at(dz=step) if kk == 0 else me.at(dy=step)
                cp = remote(part, part, s2.at[a, i, 2 + direction], r2.at[a, i, 2 + direction], peer)
                cp.start()
                ring2[a, i, 2 + direction] = cp
    for key, cp in ring2.items():
        if key[2] >= 2:
            cp.wait_recv()
    for cp in (side, g_cp, m_cp, side_low, side_high):
        cp.wait_recv()
    for cp in (x_loc, g_loc, m_loc):
        cp.wait()
    for cp in pending + [up, down, side, g_cp, m_cp, side_low, side_high]:
        cp.wait_send()
    for cp in list(ring1.values()) + list(ring2.values()):
        cp.wait_send()


def gather_inputs(wq, wo, xin, gain, meta):
    bf16 = jnp.bfloat16
    rows_q, wide_q = wq.shape[1:]
    rows_o, wide_o = wo.shape[1:]
    dma = pltpu.SemaphoreType.DMA
    return pl.pallas_call(
        gather_kernel,
        out_shape=(
            jax.ShapeDtypeStruct((2, 4, 4, 2, rows_q, wide_q), bf16),
            jax.ShapeDtypeStruct((2, 4, 4, 2, rows_o, wide_o), bf16),
            jax.ShapeDtypeStruct((2, xin.shape[0], 2 * xin.shape[1]), bf16),
            jax.ShapeDtypeStruct((2,) + gain.shape, jnp.float32),
            jax.ShapeDtypeStruct((2,) + meta.shape, jnp.int32),
        ),
        in_specs=[ANY] * 5,
        out_specs=(ANY,) * 5,
        scratch_shapes=[
            dma((2, 4)), dma((2, 4)), dma((2, 4, 4)), dma((2, 4, 4)), dma((2, 4, 4)), dma((2, 4, 4)),
            dma((7,)), dma((7,)), dma((3,)),
        ],
        compiler_params=pltpu.CompilerParams(collective_id=0, has_side_effects=True),
        name="gather_inputs",
    )(wq, wo, xin, gain, meta)


def ring_kernel(v, v_all, ss, rs, loc):
    me = Place()
    c, x = me.c, me.x
    greet([me.at(dx=1), me.at(dx=3), me.at(sibling=True)])
    rows, width = v.shape
    half = rows // 2

    def cols(xx):
        start = (c * RING + xx) * width
        return pl.ds(pl.multiple_of(start, width), width)

    low, high = pl.ds(0, half), pl.ds(half, half)
    mine = v_all.at[:, cols(x)]
    local = pltpu.make_async_copy(v, mine, loc)
    local.start()
    up = remote(v, mine, ss.at[0], rs.at[0], me.at(dx=1))
    down = remote(v, mine, ss.at[1], rs.at[1], me.at(dx=3))
    side = remote(v, mine, ss.at[2], rs.at[2], me.at(sibling=True))
    for cp in (up, down, side):
        cp.start()
    left, right, far = (lax.rem(x + j, RING) for j in (3, 1, 2))
    copies = [up, down, side]

    def forward(part, index, peer):
        cp = remote(part, part, ss.at[index], rs.at[index], peer)
        cp.start()
        copies.append(cp)
        return cp

    up.wait_recv()
    on_up = forward(v_all.at[low, cols(left)], 3, me.at(dx=1))
    waits = [side, forward(v_all.at[:, cols(left)], 5, me.at(sibling=True))]
    down.wait_recv()
    on_down = forward(v_all.at[high, cols(right)], 4, me.at(dx=3))
    waits.append(forward(v_all.at[:, cols(right)], 6, me.at(sibling=True)))
    on_up.wait_recv()
    waits.append(forward(v_all.at[low, cols(far)], 7, me.at(sibling=True)))
    on_down.wait_recv()
    waits.append(forward(v_all.at[high, cols(far)], 8, me.at(sibling=True)))
    for cp in waits:
        cp.wait_recv()
    for cp in copies:
        cp.wait_send()
    local.wait()


def ring_gather(v, ident):
    rows, width = v.shape
    dma = pltpu.SemaphoreType.DMA
    return pl.pallas_call(
        ring_kernel,
        out_shape=jax.ShapeDtypeStruct((rows, 8 * width), v.dtype),
        in_specs=[ANY],
        out_specs=ANY,
        scratch_shapes=[dma((9,)), dma((9,)), dma],
        compiler_params=pltpu.CompilerParams(collective_id=ident, has_side_effects=True),
        name="ring_gather",
    )(v)


def tail_kernel(part, skipped, w_up2, weighted, pred, grad, got, pair, ys, zs, sem_s, sem_r):
    me = Place()
    partner = {"section": me.s, "tp": me.c, "dp": me.z * 8 + me.y * 2 + 1 - me.k}
    peers_y = [me.at(dy=j) for j in (1, 2, 3)]
    peers_z = [me.at(dz=j) for j in (1, 2, 3)]
    greet([me.at(sibling=True), partner] + peers_y + peers_z)
    cp = remote(part, got, sem_s.at[0], sem_r.at[0], me.at(sibling=True))
    cp.start()
    cp.wait()
    summed = part[...].astype(jnp.float32) + got[...].astype(jnp.float32)
    value = summed + skipped[...].astype(jnp.float32)
    upper = (value / (1.0 + jnp.exp(-value))).astype(jnp.bfloat16)
    pred[...] = jnp.dot(upper, w_up2[...], preferred_element_type=jnp.float32)
    g0 = lax.dot_general(weighted[...], upper, (((0,), (0,)), ((), ())),
                         preferred_element_type=jnp.float32)
    pair[0] = g0
    cp = remote(pair.at[0], pair.at[1], sem_s.at[1], sem_r.at[1], partner)
    cp.start()
    cp.wait()
    ys[me.y] = pair[0] + pair[1]
    copies = []
    for n, peer in enumerate(peers_y):
        cp = remote(ys.at[me.y], ys.at[me.y], sem_s.at[2 + n], sem_r.at[2 + n], peer)
        cp.start()
        copies.append(cp)
    for cp in copies:
        cp.wait()
    zs[me.z] = ys[0] + ys[1] + ys[2] + ys[3]
    copies = []
    for n, peer in enumerate(peers_z):
        cp = remote(zs.at[me.z], zs.at[me.z], sem_s.at[5 + n], sem_r.at[5 + n], peer)
        cp.start()
        copies.append(cp)
    for cp in copies:
        cp.wait()
    grad[...] = zs[0] + zs[1] + zs[2] + zs[3]


def unet_tail(part, skipped, w_up2, weighted):
    rows, channels = part.shape
    wide = w_up2.shape[1]
    f32 = jnp.float32
    dma = pltpu.SemaphoreType.DMA
    return pl.pallas_call(
        tail_kernel,
        out_shape=(jax.ShapeDtypeStruct((rows, wide), f32), jax.ShapeDtypeStruct((wide, channels), f32)),
        in_specs=[VM] * 4,
        out_specs=(VM, VM),
        scratch_shapes=[
            pltpu.VMEM(part.shape, part.dtype),
            pltpu.VMEM((2, wide, channels), f32),
            pltpu.VMEM((4, wide, channels), f32),
            pltpu.VMEM((4, wide, channels), f32),
            dma((8,)), dma((8,)),
        ],
        compiler_params=pltpu.CompilerParams(collective_id=5, has_side_effects=True,
                                             vmem_limit_bytes=32 << 20),
        name="unet_tail",
    )(part, skipped, w_up2, weighted)


def allowed_pairs(meta, rows, img_tok):
    segment, start, count = meta[0], meta[1, :1], meta[2, :1]
    position = jnp.arange(rows, dtype=jnp.int32)
    in_image = (count > 0) & (position >= start) & (position < start + img_tok)
    same = segment[:, None] == segment[None, :]
    causal = position[None, :] <= position[:, None]
    return same & (causal | in_image[:, None] & in_image[None, :])


def shards(
    tokens_in, patches, segment_ids, img_start, img_count, norm_gain, w_qkv, w_out, w_down1, w_down2,
    w_up1, w_up2, cotangent,
):
    bf16, f32 = jnp.bfloat16, jnp.float32
    me = Place()
    rows, width = tokens_in.shape[1:]
    img_tok = patches.shape[1]
    depth, heads, three, hdim = w_qkv.shape[1:]
    per = heads // RING
    wide_q = per * three * hdim
    out_cols = w_out.shape[2] // RING
    wq = jnp.transpose(w_qkv[0].reshape(depth, RING, wide_q), (1, 0, 2))
    wo = jnp.transpose(w_out[0].reshape(w_out.shape[1], RING, out_cols), (1, 0, 2))

    inner = jnp.dot(patches[0], w_down1, preferred_element_type=f32)
    skipped = jax.nn.silu(inner).astype(bf16)
    image = jnp.dot(skipped, w_down2, preferred_element_type=f32).astype(bf16)
    placed = lax.dynamic_update_slice_in_dim(tokens_in[0], image, img_start[0], 0)
    x_own = jnp.where(img_count[0] > 0, placed, tokens_in[0])
    meta = jnp.concatenate(
        [segment_ids, jnp.broadcast_to(img_start[:, None], (1, rows)),
         jnp.broadcast_to(img_count[:, None], (1, rows)), jnp.zeros((5, rows), jnp.int32)], axis=0)

    q_all, o_all, x_all, gains, metas = gather_inputs(wq, wo, x_own, norm_gain, meta)
    allowed = jax.vmap(lambda m: allowed_pairs(m, rows, img_tok))(metas)
    current = x_all.reshape(2 * rows, 2 * width)
    first = (me.c * RING + me.x) * out_cols
    states = []
    for layer in (0, 1):
        weights = q_all[layer].reshape(-1, wide_q)
        values = current.astype(f32)
        mean_sq = jnp.mean(values * values, axis=-1, keepdims=True)
        normed = (values * lax.rsqrt(mean_sq + EPSILON) * gains[layer]).astype(bf16)
        proj = jnp.dot(normed, weights, preferred_element_type=f32).astype(bf16)
        proj = proj.reshape(2, rows, per, three, hdim)
        query, keys, vals = proj[:, :, :, 0], proj[:, :, :, 1], proj[:, :, :, 2]
        scores = jnp.einsum("mqhk,mshk->mhqs", query, keys, preferred_element_type=f32) / math.sqrt(hdim)
        scores = jnp.where(allowed[:, None], scores, -1e30)
        probs = jnp.exp(scores - jnp.max(scores, axis=-1, keepdims=True))
        probs = (probs / jnp.sum(probs, axis=-1, keepdims=True)).astype(bf16)
        mixed = jnp.einsum("mhqs,mshk->mqhk", probs, vals, preferred_element_type=f32).astype(bf16)
        all_heads = ring_gather(mixed.reshape(2 * rows, per * hdim), 1 + layer)
        added = jnp.dot(all_heads, o_all[layer].reshape(-1, out_cols), preferred_element_type=f32)
        mine = lax.dynamic_slice_in_dim(current, first, out_cols, 1)
        result = (mine.astype(f32) + added).astype(bf16)
        current = ring_gather(result, 3 + layer if layer == 0 else 4)
        states.append(current)

    def own_block(full):
        return lax.dynamic_slice(full, (me.k * rows, me.c * width), (rows, width))

    hidden = jnp.where(me.s == 0, own_block(states[0]), own_block(states[1]))
    final = lax.dynamic_slice(states[1], (me.k * rows + img_start[0], me.c * width), (img_tok, width))
    part = jnp.dot(final, w_up1, preferred_element_type=f32)
    weighted = jnp.where(img_count[0] > 0, cotangent[0], jnp.zeros_like(cotangent[0]))
    pred, grad = unet_tail(part, skipped, w_up2, weighted)
    pred = jnp.where(img_count[0] > 0, pred, 0.0).astype(bf16)
    return (hidden[None, None], pred[None], grad.T)


def solution(mesh):
    placed = (
        P("dp", None, "tp"),
        P("dp", None, None),
        P("dp", None),
        P("dp"),
        P("dp"),
        P("section", None),
        P("section", "dp", "tp", None, None),
        P("section", "dp", "tp"),
        P(),
        P(None, "tp"),
        P("tp", None),
        P(None, "section"),
        P("dp", None, "section"),
    )
    return jax.shard_map(
        shards,
        mesh=mesh,
        in_specs=placed,
        out_specs=(P("section", "dp", None, "tp"), P("dp", None, "section"), P(None, "section")),
        check_vma=False,
    )
```

```python
import math

import jax
import jax.numpy as jnp
from jax import lax
from jax.experimental import pallas as pl
from jax.experimental.pallas import tpu as pltpu
from jax.sharding import PartitionSpec as P

EPSILON = 1e-05
MESH = pl.DeviceIdType.MESH
ANY = pl.BlockSpec(memory_space=pl.ANY)
VM = pl.BlockSpec(memory_space=pltpu.VMEM)
RING = 4
BF16, F32 = jnp.bfloat16, jnp.float32


def dot(a, b):
    return jnp.dot(a, b, preferred_element_type=F32)


def outer(a, b):
    return lax.dot_general(a, b, (((0,), (0,)), ((), ())), preferred_element_type=F32)


class Place:
    def __init__(self):
        self.s = lax.axis_index("section")
        self.c = lax.axis_index("tp")
        d = lax.axis_index("dp")
        self.k = lax.rem(d, 2)
        self.y = lax.rem(lax.div(d, 2), RING)
        self.z = lax.div(d, 2 * RING)
        self.x = 2 * self.s + self.k

    def at(self, dx=0, dy=0, dz=0, sibling=False):
        x = lax.rem(self.x + dx, RING)
        y = lax.rem(self.y + dy, RING)
        z = lax.rem(self.z + dz, RING)
        return {
            "section": lax.div(x, 2),
            "tp": 1 - self.c if sibling else self.c,
            "dp": z * 8 + y * 2 + lax.rem(x, 2),
        }

    def partner(self):
        return {"section": self.s, "tp": self.c, "dp": self.z * 8 + self.y * 2 + 1 - self.k}


def remote(src, dst, send, recv, peer):
    return pltpu.make_async_remote_copy(
        src_ref=src, dst_ref=dst, send_sem=send, recv_sem=recv, device_id=peer, device_id_type=MESH
    )


class Spread:
    def __init__(self, me, ref, s1, r1, s2, r2):
        self.me, self.ref, self.sems = me, ref, (s1, r1, s2, r2)

    def first(self, kk, n):
        me, ref = self.me, self.ref
        s1, r1 = self.sems[:2]
        step = 1 if n % 2 == 0 else 3
        peer = me.at(dy=step) if kk == 0 else me.at(dz=step)
        if n < 2:
            part = ref.at[me.z, me.y, kk]
        else:
            back = 4 - step
            zz = me.z if kk == 0 else lax.rem(me.z + back, RING)
            yy = lax.rem(me.y + back, RING) if kk == 0 else me.y
            half = ref.shape[3] // 2
            part = ref.at[zz, yy, kk, pl.ds((n - 2) * half, half)]
        return remote(part, part, s1.at[kk, n], r1.at[kk, n], peer)

    def second(self, kk, n):
        me, ref = self.me, self.ref
        s2, r2 = self.sems[2:]
        step = 1 if n % 2 == 0 else 3
        peer = me.at(dz=step) if kk == 0 else me.at(dy=step)
        if n < 2:
            part = ref.at[me.z, :, kk] if kk == 0 else ref.at[:, me.y, kk]
        else:
            piece = pl.ds(2 * (n - 2), 2)
            back = 4 - step
            if kk == 0:
                part = ref.at[lax.rem(me.z + back, RING), piece, kk]
            else:
                part = ref.at[piece, lax.rem(me.y + back, RING), kk]
        return remote(part, part, s2.at[kk, n], r2.at[kk, n], peer)

    def own1(self):
        for kk in (0, 1):
            for n in (0, 1):
                self.first(kk, n).start()

    def pass1(self):
        for kk in (0, 1):
            for n in (0, 1):
                self.first(kk, n).wait_recv()
                self.first(kk, n + 2).start()

    def own2(self):
        for kk in (0, 1):
            for n in (2, 3):
                self.first(kk, n).wait_recv()
            for n in (0, 1):
                self.second(kk, n).start()

    def pass2(self):
        for kk in (0, 1):
            for n in (0, 1):
                self.second(kk, n).wait_recv()
                self.second(kk, n + 2).start()

    def done(self):
        for kk in (0, 1):
            for n in (2, 3):
                self.second(kk, n).wait_recv()

    def drain(self):
        for kk in (0, 1):
            for n in range(4):
                self.first(kk, n).wait_send()
                self.second(kk, n).wait_send()


class Ring:
    def __init__(self, me, ref, ss, rs):
        self.me, self.ref, self.ss, self.rs = me, ref, ss, rs

    def copy(self, n):
        me, ref = self.me, self.ref
        half = ref.shape[1] // 2

        def block(back):
            return me.c * RING + lax.rem(me.x + back, RING)

        up, down, side = me.at(dx=1), me.at(dx=3), me.at(sibling=True)
        part, peer = (
            lambda: (ref.at[block(0)], up),
            lambda: (ref.at[block(0)], down),
            lambda: (ref.at[block(0)], side),
            lambda: (ref.at[block(3), pl.ds(0, half)], up),
            lambda: (ref.at[block(1), pl.ds(half, half)], down),
            lambda: (ref.at[block(3)], side),
            lambda: (ref.at[block(1)], side),
            lambda: (ref.at[block(2)], side),
        )[n]()
        return remote(part, part, self.ss.at[n], self.rs.at[n], peer)

    def start(self):
        for n in (0, 1, 2):
            self.copy(n).start()

    def direct(self):
        self.copy(0).wait_recv()
        self.copy(3).start()
        self.copy(5).start()
        self.copy(1).wait_recv()
        self.copy(4).start()
        self.copy(6).start()

    def far(self):
        self.copy(3).wait_recv()
        self.copy(4).wait_recv()
        self.copy(7).start()

    def finish(self):
        for n in (2, 5, 6, 7):
            self.copy(n).wait_recv()

    def drain(self):
        for n in range(8):
            self.copy(n).wait_send()


def kernel(
    wq, wo_parts, wo_whole, tokens, patches, wd1, wd2, wu1, wu2, gain, meta, cot,
    hid, pred, grad,
    w_q, w_o0, w_o1, xs, heads, acc, qkv, bias, ssq, gains, metas, skip, tok, down2, up1,
    half_sum, got, upper, pair, ys, zs,
    s0q, r0q, s0o, r0o, s0w, r0w, s1, r1, s2, r2, ring_s, ring_r, sx, rx, st, rt, loc,
):
    me = Place()
    s, c, k, x, y, z = me.s, me.c, me.k, me.x, me.y, me.z
    rows = tokens.shape[0]
    img_tok = patches.shape[0]
    block = xs.shape[3]
    mine = c * RING + x
    side = me.at(sibling=True)

    loads = [
        pltpu.make_async_copy(tokens, tok, loc.at[0]),
        pltpu.make_async_copy(wd2, down2, loc.at[1]),
        pltpu.make_async_copy(wu1, up1, loc.at[2]),
        pltpu.make_async_copy(gain, gains.at[s], loc.at[3]),
        pltpu.make_async_copy(meta, metas.at[k], loc.at[4]),
    ]
    for cp in loads:
        cp.start()

    peers = ([me.at(dx=j) for j in (1, 2, 3)] + [me.at(dy=j) for j in (1, 2, 3)]
             + [me.at(dz=j) for j in (1, 2, 3)] + [side])
    barrier = pltpu.get_barrier_semaphore()
    for peer in peers:
        pl.semaphore_signal(barrier, inc=1, device_id=peer, device_id_type=MESH)
    pl.semaphore_wait(barrier, len(peers))

    def scatter_q(j):
        return remote(wq.at[lax.rem(x + j, RING)], w_q.at[s, z, y, k], s0q.at[j], r0q.at[x], me.at(dx=j))

    def scatter_o(j):
        return remote(wo_parts.at[lax.rem(x + j, RING)], w_o0.at[z, y, k], s0o.at[j], r0o.at[k],
                      me.at(dx=j))

    def whole_o():
        return remote(wo_whole, w_o1.at[z, y, k], s0w.at[0], r0w.at[k], me.partner())

    for j in (1, 2, 3):
        scatter_q(j).start()
    pltpu.make_async_copy(wq.at[x], w_q.at[s, z, y, k], r0q.at[x]).start()

    @pl.when(s == 0)
    def _():
        for j in (1, 2, 3):
            scatter_o(j).start()
        pltpu.make_async_copy(wo_parts.at[x], w_o0.at[z, y, k], r0o.at[k]).start()

    @pl.when(s == 1)
    def _():
        whole_o().start()
        pltpu.make_async_copy(wo_whole, w_o1.at[z, y, k], r0w.at[k]).start()

    for cp in loads:
        cp.wait()
    g_cp = remote(gains.at[s], gains.at[s], sx.at[3], rx.at[3], me.at(dx=2))
    m_cp = remote(metas.at[k], metas.at[k], sx.at[4], rx.at[4], me.at(dx=1))
    g_cp.start()
    m_cp.start()

    inner = dot(patches[...], wd1[...])
    skip[...] = (inner / (1.0 + jnp.exp(-inner))).astype(BF16)
    own_start, own_count = metas[k, 1:2, :], metas[k, 2:3, :]
    rr = lax.broadcasted_iota(jnp.int32, (rows, img_tok), 0)
    ii = lax.broadcasted_iota(jnp.int32, (rows, img_tok), 1)
    put = (rr == ii + own_start[:, :img_tok]).astype(F32).astype(BF16)
    rb = lax.broadcasted_iota(jnp.int32, (rows, block), 0)
    here = (rb >= own_start) & (rb < own_start + img_tok) & (own_count > 0)
    for j in range(RING):
        image = dot(skip[...], down2[:, j * block:(j + 1) * block]).astype(BF16)
        moved = dot(put, image)
        old = tok[:, j * block:(j + 1) * block].astype(F32)
        xs[k, c * RING + j] = jnp.where(here, moved, old).astype(BF16)

    own = pl.ds(c * RING, RING)
    low, high = pl.ds(0, rows // 2), pl.ds(rows // 2, rows // 2)

    def x0_copy(n):
        if n == 0:
            part, peer = xs.at[k, own, low], me.at(dx=1)
        elif n == 1:
            part, peer = xs.at[k, own, high], me.at(dx=3)
        elif n == 2:
            part, peer = xs.at[k, own], side
        elif n == 5:
            part, peer = xs.at[1 - k, own, low], side
        else:
            part, peer = xs.at[1 - k, own, high], side
        return remote(part, part, sx.at[n], rx.at[n], peer)

    for n in (0, 1, 2):
        x0_copy(n).start()

    group = [Spread(me, ref, s1.at[i], r1.at[i], s2.at[i], r2.at[i])
             for i, ref in enumerate((w_q.at[0], w_o0, w_q.at[1], w_o1))]
    q0, o0, q1, o1 = group

    def landed(ref, sem):
        pltpu.make_async_copy(ref, ref, sem).wait()

    for kk in (0, 1):
        landed(w_q.at[0, z, y, kk], r0q.at[kk])
        landed(w_o0.at[z, y, kk], r0o.at[kk])
    q0.own1()
    o0.own1()

    def mask_of(m):
        segment, start, count = metas[m, 0:1, :], metas[m, 1:2, :], metas[m, 2:3, :]
        one_hot = (lax.broadcasted_iota(jnp.int32, (8, rows), 0) == segment).astype(F32).astype(BF16)
        same = outer(one_hot, one_hot)
        i = lax.broadcasted_iota(jnp.int32, (rows, rows), 0)
        j = lax.broadcasted_iota(jnp.int32, (rows, rows), 1)
        in_i = (i >= start) & (i < start + img_tok) & (count > 0)
        in_j = (j >= start) & (j < start + img_tok)
        ok = (same > 0.5) & ((j <= i) | (in_i & in_j))
        bias[m] = jnp.where(ok, 0.0, -1e30)

    q0.pass1()
    o0.pass1()
    m_cp.wait_recv()
    g_cp.wait_recv()
    q0.own2()
    o0.own2()
    mask_of(0)
    x0_copy(0).wait_recv()
    x0_copy(5).start()
    x0_copy(1).wait_recv()
    x0_copy(6).start()
    mask_of(1)
    for n in (2, 5, 6):
        x0_copy(n).wait_recv()
    for n in (0, 1, 2, 5, 6):
        x0_copy(n).wait_send()
    q0.pass2()
    o0.pass2()
    q0.done()
    o0.done()
    for kk in (0, 1):
        landed(w_q.at[1, z, y, kk], r0q.at[2 + kk])
    q1.own1()

    def project(layer, m):
        acc[...] = jnp.zeros_like(acc)
        ssq[...] = jnp.zeros_like(ssq)

        def body(b, carry):
            values = xs[m, b].astype(F32)
            ssq[...] += jnp.sum(values * values, axis=1, keepdims=True)
            scaled = (values * gains[layer, b]).astype(BF16)
            weights = w_q[layer, lax.div(b, 2), pl.ds(2 * lax.rem(b, 2), 2)]
            acc[...] += dot(scaled, weights.reshape(block, acc.shape[1]))
            return carry

        lax.fori_loop(0, 2 * RING, body, 0)
        scale = lax.rsqrt(ssq[...] * (1.0 / (2 * RING * block)) + EPSILON)
        qkv[m] = (acc[...] * scale).astype(BF16)

    hdim = 128
    per = heads.shape[4] // hdim
    q_rows = 128

    def attend(layer, m):
        def body(i, carry):
            at = pl.ds(pl.multiple_of(i * q_rows, q_rows), q_rows)
            for h in range(per):
                base = 3 * h * hdim
                query = qkv[m, at, base:base + hdim]
                keys = qkv[m, :, base + hdim:base + 2 * hdim]
                vals = qkv[m, :, base + 2 * hdim:base + 3 * hdim]
                scores = lax.dot_general(query, keys, (((1,), (1,)), ((), ())), preferred_element_type=F32)
                scores = scores * (1.0 / math.sqrt(hdim)) + bias[m, at, :]
                probs = jnp.exp(scores - jnp.max(scores, axis=1, keepdims=True))
                probs = (probs / jnp.sum(probs, axis=1, keepdims=True)).astype(BF16)
                heads[layer, m, mine, at, h * hdim:(h + 1) * hdim] = dot(probs, vals).astype(BF16)
            return carry

        lax.fori_loop(0, rows // q_rows, body, 0)

    h_ring = [[Ring(me, heads.at[layer, m], ring_s.at[layer, m], ring_r.at[layer, m]) for m in (0, 1)]
              for layer in (0, 1)]
    x_ring = [Ring(me, xs.at[m], ring_s.at[2, m], ring_r.at[2, m]) for m in (0, 1)]

    def mix0(m):
        half_sum[...] = jnp.zeros_like(half_sum)

        def body(b, carry):
            weights = w_o0[lax.div(b, 2), pl.ds(2 * lax.rem(b, 2), 2)]
            half_sum[...] += dot(heads[0, m, b], weights.reshape(per * hdim, block))
            return carry

        lax.fori_loop(0, 2 * RING, body, 0)
        xs[m, mine] = (xs[m, mine].astype(F32) + half_sum[...]).astype(BF16)

    def section_one(act):
        pl.when(s == 1)(act)

    project(0, 0)
    q1.pass1()
    project(0, 1)
    q1.own2()
    attend(0, 0)
    h_ring[0][0].start()
    attend(0, 1)
    h_ring[0][1].start()
    h_ring[0][0].direct()
    h_ring[0][0].far()
    h_ring[0][0].finish()
    mix0(0)
    x_ring[0].start()
    q1.pass2()

    def start_o1():
        for kk in (0, 1):
            landed(w_o1.at[z, y, kk], r0w.at[kk])
        o1.own1()

    section_one(start_o1)
    h_ring[0][1].direct()
    h_ring[0][1].far()
    h_ring[0][1].finish()
    mix0(1)
    x_ring[1].start()
    section_one(o1.pass1)
    x_ring[0].direct()
    section_one(o1.own2)
    x_ring[0].far()
    x_ring[0].finish()
    q1.done()
    x_ring[1].direct()
    project(1, 0)
    attend(1, 0)
    h_ring[1][0].start()
    x_ring[1].far()
    x_ring[1].finish()
    project(1, 1)
    section_one(o1.pass2)
    attend(1, 1)
    h_ring[1][1].start()

    def put_first(j):
        return pltpu.make_async_copy(xs.at[k, c * RING + j], hid.at[:, pl.ds(j * block, block)], loc.at[j])

    @pl.when(s == 0)
    def _():
        for j in range(RING):
            put_first(j).start()

    h_ring[1][0].direct()
    h_ring[1][0].far()
    h_ring[1][1].direct()
    h_ring[1][1].far()
    h_ring[1][0].finish()
    h_ring[1][1].finish()

    def put_last(j):
        return pltpu.make_async_copy(tok.at[:, pl.ds(j * block, block)], hid.at[:, pl.ds(j * block, block)],
                                     loc.at[j])

    def tail_copy(n):
        if n == 0:
            return remote(half_sum.at[pl.ds(0, img_tok)], got, st.at[0], rt.at[0], side)
        if n == 1:
            return remote(upper, upper, st.at[1], rt.at[1], me.at(dx=2))
        if n == 2:
            return remote(pair.at[0], pair.at[1], st.at[2], rt.at[2], me.partner())
        if n < 6:
            return remote(ys.at[y], ys.at[y], st.at[n], rt.at[n], me.at(dy=n - 2))
        return remote(zs.at[z], zs.at[z], st.at[n], rt.at[n], me.at(dz=n - 5))

    @pl.when(s == 1)
    def _():
        o1.done()
        for j in range(RING):
            half_sum[...] = jnp.zeros_like(half_sum)

            def body(b, carry):
                weights = w_o1[lax.div(b, 2), pl.ds(2 * lax.rem(b, 2), 2), :, :, j * block:(j + 1) * block]
                half_sum[...] += dot(heads[1, k, b], weights.reshape(per * hdim, block))
                return carry

            lax.fori_loop(0, 2 * RING, body, 0)
            old = xs[k, c * RING + j].astype(F32)
            tok[:, j * block:(j + 1) * block] = (old + half_sum[...]).astype(BF16)
            put_last(j).start()
        ri = lax.broadcasted_iota(jnp.int32, (img_tok, rows), 0)
        ci = lax.broadcasted_iota(jnp.int32, (img_tok, rows), 1)
        take = (ci == ri + metas[k, 1:2, :]).astype(F32).astype(BF16)
        total = jnp.zeros((img_tok, up1.shape[1]), F32)
        for j in range(RING):
            final = dot(take, tok[:, j * block:(j + 1) * block]).astype(BF16)
            total = total + dot(final, up1[j * block:(j + 1) * block, :])
        half_sum[0:img_tok, :] = total
        tail_copy(0).start()
        tail_copy(0).wait_recv()
        value = half_sum[0:img_tok, :] + got[...] + skip[...].astype(F32)
        upper[...] = (value / (1.0 + jnp.exp(-value))).astype(BF16)
        tail_copy(1).start()
        tail_copy(0).wait_send()
        for j in range(RING):
            put_last(j).wait()

    @pl.when(s == 0)
    def _():
        for j in range(RING):
            put_first(j).wait()
        tail_copy(1).wait_recv()

    present = metas[k, 2:3, :wu2.shape[1]] > 0
    weighted = jnp.where(present, cot[...].astype(F32), 0.0).astype(BF16)
    pred[...] = jnp.where(present, dot(upper[...], wu2[...]), 0.0).astype(BF16)
    pair[0] = outer(weighted, upper[...])
    tail_copy(2).start()
    tail_copy(2).wait()
    ys[y] = pair[0] + pair[1]
    for n in (3, 4, 5):
        tail_copy(n).start()
    for n in (3, 4, 5):
        tail_copy(n).wait()
    zs[z] = ys[0] + ys[1] + ys[2] + ys[3]
    for n in (6, 7, 8):
        tail_copy(n).start()
    for n in (6, 7, 8):
        tail_copy(n).wait()
    grad[...] = zs[0] + zs[1] + zs[2] + zs[3]

    for j in (1, 2, 3):
        scatter_q(j).wait_send()

    @pl.when(s == 0)
    def _():
        for j in (1, 2, 3):
            scatter_o(j).wait_send()

    @pl.when(s == 1)
    def _():
        whole_o().wait_send()
        o1.drain()
        tail_copy(1).wait_send()

    g_cp.wait_send()
    m_cp.wait_send()
    for g in (q0, o0, q1):
        g.drain()
    for r in h_ring[0] + h_ring[1] + x_ring:
        r.drain()


def window(wq, wo_parts, wo_whole, tokens, patches, wd1, wd2, wu1, wu2, gain, meta, cot):
    rows, width = tokens.shape
    block = width // RING
    depth, wide_q = wq.shape[1:]
    depth_o = wo_whole.shape[0]
    img_tok = patches.shape[0]
    channels = wd1.shape[1]
    pix = wu2.shape[1]
    head_cols = wide_q // 3
    dma = pltpu.SemaphoreType.DMA
    vm = pltpu.VMEM
    scratch = [
        vm((2, RING, RING, 2, depth, wide_q), BF16),
        vm((RING, RING, 2, depth_o, block), BF16),
        vm((RING, RING, 2, depth_o, width), BF16),
        vm((2, 2 * RING, rows, block), BF16),
        vm((2, 2, 2 * RING, rows, head_cols), BF16),
        vm((rows, wide_q), F32),
        vm((2, rows, wide_q), BF16),
        vm((2, rows, rows), F32),
        vm((rows, 1), F32),
        vm((2,) + gain.shape, F32),
        vm((2,) + meta.shape, jnp.int32),
        vm((img_tok, channels), BF16),
        vm((rows, width), BF16),
        vm(wd2.shape, BF16),
        vm(wu1.shape, BF16),
        vm((rows, block), F32),
        vm((img_tok, channels), F32),
        vm((img_tok, channels), BF16),
        vm((2, pix, channels), F32),
        vm((RING, pix, channels), F32),
        vm((RING, pix, channels), F32),
        dma((4,)), dma((4,)), dma((4,)), dma((2,)), dma((1,)), dma((2,)),
        dma((4, 2, 4)), dma((4, 2, 4)), dma((4, 2, 4)), dma((4, 2, 4)),
        dma((3, 2, 8)), dma((3, 2, 8)), dma((7,)), dma((7,)), dma((9,)), dma((9,)), dma((5,)),
    ]
    return pl.pallas_call(
        kernel,
        out_shape=(
            jax.ShapeDtypeStruct((rows, width), BF16),
            jax.ShapeDtypeStruct((img_tok, pix), BF16),
            jax.ShapeDtypeStruct((pix, channels), F32),
        ),
        in_specs=[ANY, ANY, ANY, ANY, VM, VM, ANY, ANY, VM, ANY, ANY, VM],
        out_specs=(ANY, VM, VM),
        scratch_shapes=scratch,
        compiler_params=pltpu.CompilerParams(collective_id=0, has_side_effects=True,
                                             vmem_limit_bytes=63 << 20),
        name="window",
    )(wq, wo_parts, wo_whole, tokens, patches, wd1, wd2, wu1, wu2, gain, meta, cot)


def shards(
    tokens_in, patches, segment_ids, img_start, img_count, norm_gain, w_qkv, w_out, w_down1, w_down2,
    w_up1, w_up2, cotangent,
):
    rows, width = tokens_in.shape[1:]
    depth, heads, three, hdim = w_qkv.shape[1:]
    wide_q = heads // RING * three * hdim
    block = width // RING
    wq = jnp.transpose(w_qkv[0].reshape(depth, RING, wide_q), (1, 0, 2))
    wo = jnp.transpose(w_out[0].reshape(w_out.shape[1], RING, block), (1, 0, 2))
    meta = jnp.concatenate(
        [segment_ids, jnp.broadcast_to(img_start[:, None], (1, rows)),
         jnp.broadcast_to(img_count[:, None], (1, rows)), jnp.zeros((5, rows), jnp.int32)], axis=0)
    gain = norm_gain.reshape(2 * RING, 1, block)
    hidden, pred, grad = window(wq, wo, w_out[0], tokens_in[0], patches[0], w_down1, w_down2, w_up1,
                                w_up2, gain, meta, cotangent[0])
    return (hidden[None, None], pred[None], grad.T)


def solution(mesh):
    placed = (
        P("dp", None, "tp"),
        P("dp", None, None),
        P("dp", None),
        P("dp"),
        P("dp"),
        P("section", None),
        P("section", "dp", "tp", None, None),
        P("section", "dp", "tp"),
        P(),
        P(None, "tp"),
        P("tp", None),
        P(None, "section"),
        P("dp", None, "section"),
    )
    return jax.shard_map(
        shards,
        mesh=mesh,
        in_specs=placed,
        out_specs=(P("section", "dp", None, "tp"), P("dp", None, "section"), P(None, "section")),
        check_vma=False,
    )
```

```python
import math

import jax
import jax.numpy as jnp
from jax import lax
from jax.experimental import pallas as pl
from jax.experimental.pallas import tpu as pltpu
from jax.sharding import PartitionSpec as P

EPSILON = 1e-05
MESH = pl.DeviceIdType.MESH
ANY = pl.BlockSpec(memory_space=pl.ANY)
VM = pl.BlockSpec(memory_space=pltpu.VMEM)
RING = 4
BF16, F32 = jnp.bfloat16, jnp.float32


def dot(a, b):
    return jnp.dot(a, b, preferred_element_type=F32)


def outer(a, b):
    return lax.dot_general(a, b, (((0,), (0,)), ((), ())), preferred_element_type=F32)


class Place:
    def __init__(self):
        self.s = lax.axis_index("section")
        self.c = lax.axis_index("tp")
        d = lax.axis_index("dp")
        self.k = lax.rem(d, 2)
        self.y = lax.rem(lax.div(d, 2), RING)
        self.z = lax.div(d, 2 * RING)
        self.x = 2 * self.s + self.k

    def at(self, dx=0, dy=0, dz=0, sibling=False):
        x = lax.rem(self.x + dx, RING)
        y = lax.rem(self.y + dy, RING)
        z = lax.rem(self.z + dz, RING)
        return {
            "section": lax.div(x, 2),
            "tp": 1 - self.c if sibling else self.c,
            "dp": z * 8 + y * 2 + lax.rem(x, 2),
        }

    def partner(self):
        return {"section": self.s, "tp": self.c, "dp": self.z * 8 + self.y * 2 + 1 - self.k}


def remote(src, dst, send, recv, peer):
    return pltpu.make_async_remote_copy(
        src_ref=src, dst_ref=dst, send_sem=send, recv_sem=recv, device_id=peer, device_id_type=MESH
    )


class Spread:
    def __init__(self, me, ref, s1, r1, s2, r2):
        self.me, self.ref, self.sems = me, ref, (s1, r1, s2, r2)

    def first(self, kk, n):
        me, ref = self.me, self.ref
        s1, r1 = self.sems[:2]
        step = 1 if n % 2 == 0 else 3
        peer = me.at(dy=step) if kk == 0 else me.at(dz=step)
        if n < 2:
            part = ref.at[me.z, me.y, kk]
        else:
            back = 4 - step
            zz = me.z if kk == 0 else lax.rem(me.z + back, RING)
            yy = lax.rem(me.y + back, RING) if kk == 0 else me.y
            half = ref.shape[3] // 2
            part = ref.at[zz, yy, kk, pl.ds((n - 2) * half, half)]
        return remote(part, part, s1.at[kk, n], r1.at[kk, n], peer)

    def second(self, kk, n):
        me, ref = self.me, self.ref
        s2, r2 = self.sems[2:]
        step = 1 if n % 2 == 0 else 3
        peer = me.at(dz=step) if kk == 0 else me.at(dy=step)
        if n < 2:
            part = ref.at[me.z, :, kk] if kk == 0 else ref.at[:, me.y, kk]
        else:
            piece = pl.ds(2 * (n - 2), 2)
            back = 4 - step
            if kk == 0:
                part = ref.at[lax.rem(me.z + back, RING), piece, kk]
            else:
                part = ref.at[piece, lax.rem(me.y + back, RING), kk]
        return remote(part, part, s2.at[kk, n], r2.at[kk, n], peer)

    def own1(self):
        for kk in (0, 1):
            for n in (0, 1):
                self.first(kk, n).start()

    def pass1(self):
        for kk in (0, 1):
            for n in (0, 1):
                self.first(kk, n).wait_recv()
                self.first(kk, n + 2).start()

    def own2(self):
        for kk in (0, 1):
            for n in (2, 3):
                self.first(kk, n).wait_recv()
            for n in (0, 1):
                self.second(kk, n).start()

    def pass2(self):
        for kk in (0, 1):
            for n in (0, 1):
                self.second(kk, n).wait_recv()
                self.second(kk, n + 2).start()

    def done(self):
        for kk in (0, 1):
            for n in (2, 3):
                self.second(kk, n).wait_recv()

    def drain(self):
        for kk in (0, 1):
            for n in range(4):
                self.first(kk, n).wait_send()
                self.second(kk, n).wait_send()


class Ring:
    def __init__(self, me, ref, ss, rs):
        self.me, self.ref, self.ss, self.rs = me, ref, ss, rs

    def copy(self, n):
        me, ref = self.me, self.ref
        half = ref.shape[1] // 2

        def block(back):
            return me.c * RING + lax.rem(me.x + back, RING)

        up, down, side = me.at(dx=1), me.at(dx=3), me.at(sibling=True)
        part, peer = (
            lambda: (ref.at[block(0)], up),
            lambda: (ref.at[block(0)], down),
            lambda: (ref.at[block(0)], side),
            lambda: (ref.at[block(3), pl.ds(0, half)], up),
            lambda: (ref.at[block(1), pl.ds(half, half)], down),
            lambda: (ref.at[block(3)], side),
            lambda: (ref.at[block(1)], side),
            lambda: (ref.at[block(2)], side),
        )[n]()
        return remote(part, part, self.ss.at[n], self.rs.at[n], peer)

    def start(self):
        for n in (0, 1, 2):
            self.copy(n).start()

    def direct(self):
        self.copy(0).wait_recv()
        self.copy(3).start()
        self.copy(5).start()
        self.copy(1).wait_recv()
        self.copy(4).start()
        self.copy(6).start()

    def far(self):
        self.copy(3).wait_recv()
        self.copy(4).wait_recv()
        self.copy(7).start()

    def finish(self):
        for n in (2, 5, 6, 7):
            self.copy(n).wait_recv()

    def drain(self):
        for n in range(8):
            self.copy(n).wait_send()


def kernel(
    wq, wo, tokens, patches_t, wd1, wd2, wu1, wu2_t, gain, segment, start_in, count_in, cot_t,
    hid, pred, grad,
    w_q, w_o0, w_o1, xs, heads, acc, qkv, bias, ssq, gains, metas, skip, down2, up1,
    part, got, upper, cots, ups, p_own, p_in, g_own, g_in, pair, ys, zs,
    s0q, r0q, s0o, r0o, s0w, r0w, s1, r1, s2, r2, ring_s, ring_r, sx, rx, st, rt, loc,
):
    me = Place()
    s, c, k, x, y, z = me.s, me.c, me.k, me.x, me.y, me.z
    rows = tokens.shape[0]
    img_tok = patches_t.shape[1]
    block = xs.shape[3]
    mine = c * RING + x
    side = me.at(sibling=True)

    loads = [
        pltpu.make_async_copy(tokens, hid, loc.at[0]),
        pltpu.make_async_copy(wd2, down2, loc.at[1]),
        pltpu.make_async_copy(wu1, up1, loc.at[2]),
        pltpu.make_async_copy(gain, gains.at[s], loc.at[3]),
    ]
    for cp in loads:
        cp.start()
    metas[k, 0:1, :] = segment[...]
    metas[k, 1:2, :] = jnp.full((1, rows), start_in[0], jnp.int32)
    metas[k, 2:3, :] = jnp.full((1, rows), count_in[0], jnp.int32)
    metas[k, 3:8, :] = jnp.zeros((5, rows), jnp.int32)

    peers = ([me.at(dx=j) for j in (1, 2, 3)] + [me.at(dy=j) for j in (1, 2, 3)]
             + [me.at(dz=j) for j in (1, 2, 3)] + [side])
    across = dict(me.at(dx=2), tp=1 - c)
    barrier = pltpu.get_barrier_semaphore()
    for peer in peers + [across]:
        pl.semaphore_signal(barrier, inc=1, device_id=peer, device_id_type=MESH)
    pl.semaphore_wait(barrier, len(peers) + 1)

    def scatter_q(j):
        return remote(wq.at[lax.rem(x + j, RING)], w_q.at[s, z, y, k], s0q.at[j], r0q.at[x], me.at(dx=j))

    def scatter_o(j):
        cols = pl.ds(pl.multiple_of(lax.rem(x + j, RING) * block, block), block)
        return remote(wo.at[:, cols], w_o0.at[z, y, k], s0o.at[j], r0o.at[k], me.at(dx=j))

    def whole_o():
        return remote(wo, w_o1.at[z, y, k], s0w.at[0], r0w.at[k], me.partner())

    def start_q():
        for j in (1, 3, 2):
            scatter_q(j).start()
        pltpu.make_async_copy(wq.at[x], w_q.at[s, z, y, k], r0q.at[x]).start()

    def start_o():
        for j in (1, 3, 2):
            scatter_o(j).start()
        own_cols = pl.ds(pl.multiple_of(x * block, block), block)
        pltpu.make_async_copy(wo.at[:, own_cols], w_o0.at[z, y, k], r0o.at[k]).start()

    def start_w():
        whole_o().start()
        pltpu.make_async_copy(wo, w_o1.at[z, y, k], r0w.at[k]).start()

    section_zero, section_one = pl.when(s == 0), pl.when(s == 1)
    section_zero(start_q)

    for cp in loads:
        cp.wait()
    g_cp = remote(gains.at[s], gains.at[s], sx.at[3], rx.at[3], me.at(dx=2))
    m_cp = remote(metas.at[k], metas.at[k], sx.at[4], rx.at[4], me.at(dx=1))
    g_cp.start()
    m_cp.start()

    def give(n):
        src, dst = ((cot_t, cots), (wu2_t, ups))[n - 7]
        return remote(src, dst, sx.at[n], rx.at[n], me.at(dx=2))

    @pl.when((s == 0) & (c == 0))
    def _():
        give(7).start()
        give(8).start()

    @pl.when((s == 1) & (c == 1))
    def _():
        cots[...] = cot_t[...]
        ups[...] = wu2_t[...]

    inner = outer(patches_t[...], wd1[...])
    skip[...] = (inner / (1.0 + jnp.exp(-inner))).astype(BF16)
    own_start, own_count = metas[k, 1:2, :], metas[k, 2:3, :]
    rr = lax.broadcasted_iota(jnp.int32, (rows, img_tok), 0)
    ii = lax.broadcasted_iota(jnp.int32, (rows, img_tok), 1)
    put = (rr == ii + own_start[:, :img_tok]).astype(F32).astype(BF16)
    rb = lax.broadcasted_iota(jnp.int32, (rows, block), 0)
    here = (rb >= own_start) & (rb < own_start + img_tok) & (own_count > 0)
    for j in range(RING):
        image = dot(skip[...], down2[:, j * block:(j + 1) * block]).astype(BF16)
        moved = dot(put, image)
        old = hid[:, j * block:(j + 1) * block].astype(F32)
        xs[k, c * RING + j] = jnp.where(here, moved, old).astype(BF16)

    own = pl.ds(c * RING, RING)
    low, high = pl.ds(0, rows // 2), pl.ds(rows // 2, rows // 2)

    def x0_copy(n):
        if n == 0:
            what, peer = xs.at[k, own, low], me.at(dx=1)
        elif n == 1:
            what, peer = xs.at[k, own, high], me.at(dx=3)
        elif n == 2:
            what, peer = xs.at[k, own], side
        elif n == 5:
            what, peer = xs.at[1 - k, own, low], side
        else:
            what, peer = xs.at[1 - k, own, high], side
        return remote(what, what, sx.at[n], rx.at[n], peer)

    group = [Spread(me, ref, s1.at[i], r1.at[i], s2.at[i], r2.at[i])
             for i, ref in enumerate((w_q.at[0], w_o0, w_q.at[1], w_o1))]
    q0, o0, q1, o1 = group

    def landed(ref, sem):
        pltpu.make_async_copy(ref, ref, sem).wait()

    def mask_of(m):
        segment, start, count = metas[m, 0:1, :], metas[m, 1:2, :], metas[m, 2:3, :]
        one_hot = (lax.broadcasted_iota(jnp.int32, (8, rows), 0) == segment).astype(F32).astype(BF16)
        same = outer(one_hot, one_hot)
        i = lax.broadcasted_iota(jnp.int32, (rows, rows), 0)
        j = lax.broadcasted_iota(jnp.int32, (rows, rows), 1)
        in_i = (i >= start) & (i < start + img_tok) & (count > 0)
        in_j = (j >= start) & (j < start + img_tok)
        ok = (same > 0.5) & ((j <= i) | (in_i & in_j))
        bias[m] = jnp.where(ok, 0.0, -1e30)

    for kk in (0, 1):
        landed(w_q.at[0, z, y, kk], r0q.at[kk])
    q0.own1()
    for n in (0, 1, 2):
        x0_copy(n).start()
    section_zero(start_o)
    q0.pass1()
    m_cp.wait_recv()
    g_cp.wait_recv()
    mask_of(0)
    q0.own2()
    mask_of(1)
    x0_copy(0).wait_recv()
    x0_copy(5).start()
    x0_copy(1).wait_recv()
    x0_copy(6).start()

    @section_one
    def _():
        start_q()
        start_w()

    q0.pass2()
    for kk in (0, 1):
        landed(w_o0.at[z, y, kk], r0o.at[kk])
    o0.own1()
    for n in (2, 5, 6):
        x0_copy(n).wait_recv()

    def band(m, step, first=False):
        pieces, squares = [], 0.0
        zz, yy = lax.rem(z + step, RING), lax.rem(y + step, RING)

        def take(b, at):
            values = xs[m, b, :, at].astype(F32)
            pieces.append((values * gains[0, b, :, at]).astype(BF16))
            return jnp.sum(values * values, axis=1, keepdims=True)

        half = block // 2
        depth = half // 2
        for b in (0, 1):
            for at in (0, half):
                squares += take(2 * zz + b, slice(at, at + depth))
        for b in range(RING):
            at = pl.ds(pl.multiple_of(lax.rem(yy, 2) * half + depth, depth), depth)
            squares += take(2 * b + lax.div(yy, 2), at)
        weights = jnp.concatenate(
            [w_q[0, zz, :, 0].reshape(block, acc.shape[2]), w_q[0, :, yy, 1].reshape(block, acc.shape[2])], axis=0)
        total = dot(jnp.concatenate(pieces, axis=1), weights)
        if first:
            acc[m] = total
            ssq[m] = squares
        else:
            acc[m] += total
            ssq[m] += squares

    def scaled(m):
        scale = lax.rsqrt(ssq[m] * (1.0 / (2 * RING * block)) + EPSILON)
        qkv[m] = (acc[m] * scale).astype(BF16)

    def project1(m):
        ssq[m] = jnp.zeros_like(ssq[m])
        for b in range(0, 2 * RING, 2):
            pieces = []
            for n in (b, b + 1):
                values = xs[m, n].astype(F32)
                ssq[m] += jnp.sum(values * values, axis=1, keepdims=True)
                pieces.append((values * gains[1, n]).astype(BF16))
            total = dot(jnp.concatenate(pieces, axis=1), w_q[1, b // 2].reshape(2 * block, acc.shape[2]))
            if b == 0:
                acc[m] = total
            else:
                acc[m] += total
        scaled(m)

    hdim = 128
    per = heads.shape[3] // hdim
    q_rows = 128

    def attend(layer, m):
        for i in range(rows // q_rows):
            at = pl.ds(i * q_rows, q_rows)
            for h in range(per):
                base = 3 * h * hdim
                query = qkv[m, at, base:base + hdim]
                keys = qkv[m, :, base + hdim:base + 2 * hdim]
                vals = qkv[m, :, base + 2 * hdim:base + 3 * hdim]
                scores = lax.dot_general(query, keys, (((1,), (1,)), ((), ())), preferred_element_type=F32)
                scores = scores * (1.0 / math.sqrt(hdim)) + bias[m, at, :]
                probs = jnp.exp(scores - jnp.max(scores, axis=1, keepdims=True))
                probs = (probs * (1.0 / jnp.sum(probs, axis=1, keepdims=True))).astype(BF16)
                heads[m, mine, at, h * hdim:(h + 1) * hdim] = dot(probs, vals).astype(BF16)

    h_ring = [[Ring(me, heads.at[m], ring_s.at[layer, m], ring_r.at[layer, m]) for m in (0, 1)]
              for layer in (0, 1)]
    x_ring = [Ring(me, xs.at[m], ring_s.at[2, m], ring_r.at[2, m]) for m in (0, 1)]

    def mix0(m):
        together = jnp.concatenate([heads[m, b] for b in range(2 * RING)], axis=1)
        added = dot(together, w_o0[...].reshape(2 * RING * per * hdim, block))
        xs[m, mine] = (xs[m, mine].astype(F32) + added).astype(BF16)

    for step in (0, 1, 3):
        for m in (0, 1):
            band(m, step, step == 0)
    for n in (0, 1, 2, 5, 6):
        x0_copy(n).wait_send()
    q0.done()
    o0.pass1()
    band(0, 2)
    scaled(0)
    attend(0, 0)
    h_ring[0][0].start()
    o0.own2()
    band(1, 2)
    scaled(1)
    attend(0, 1)
    h_ring[0][1].start()
    o0.pass2()
    for kk in (0, 1):
        landed(w_q.at[1, z, y, kk], r0q.at[2 + kk])
    q1.own1()
    h_ring[0][0].direct()
    h_ring[0][0].far()
    h_ring[0][0].finish()
    o0.done()
    mix0(0)
    h_ring[0][0].drain()
    x_ring[0].start()
    q1.pass1()
    h_ring[0][1].direct()
    h_ring[0][1].far()
    h_ring[0][1].finish()
    mix0(1)
    h_ring[0][1].drain()
    x_ring[1].start()
    q1.own2()

    @section_one
    def _():
        for kk in (0, 1):
            landed(w_o1.at[z, y, kk], r0w.at[kk])
        o1.own1()

    x_ring[0].direct()
    x_ring[0].far()
    section_one(o1.pass1)
    q1.pass2()
    section_one(o1.own2)
    x_ring[0].finish()
    x_ring[1].direct()
    q1.done()
    project1(0)
    attend(1, 0)
    h_ring[1][0].start()
    x_ring[1].far()
    section_one(o1.pass2)
    x_ring[1].finish()
    project1(1)
    h_ring[1][0].direct()
    attend(1, 1)
    h_ring[1][1].start()

    @section_zero
    def _():
        for j in range(RING):
            hid[:, j * block:(j + 1) * block] = xs[k, c * RING + j]

    h_ring[1][0].far()
    h_ring[1][1].direct()
    h_ring[1][1].far()
    h_ring[1][0].finish()
    h_ring[1][1].finish()

    def tail_copy(n):
        if n == 0:
            return remote(part, got, st.at[0], rt.at[0], side)
        if n == 2:
            return remote(pair.at[0], pair.at[1], st.at[2], rt.at[2], me.partner())
        if n < 6:
            return remote(ys.at[y], ys.at[y], st.at[n], rt.at[n], me.at(dy=n - 2))
        return remote(zs.at[z], zs.at[z], st.at[n], rt.at[n], me.at(dz=n - 5))

    def result_copy(n, core):
        src, dst = ((p_own, p_in), (g_own, g_in))[n]
        peer = side if core is None else dict(me.at(dx=2), tp=core)
        index = 0 if core is None else core
        return remote(src, dst, st.at[9 + 2 * n + index], rt.at[9 + n], peer)

    def send_result(n):
        @pl.when(c == 0)
        def _():
            result_copy(n, 0).start()
            result_copy(n, 1).start()

        @pl.when(c == 1)
        def _():
            result_copy(n, None).start()

    @section_one
    def _():
        @pl.when(c == 0)
        def _():
            give(7).wait_recv()
            give(8).wait_recv()

        o1.done()
        together = jnp.concatenate([heads[k, b] for b in range(2 * RING)], axis=1)
        for j in range(RING):
            at = slice(j * block, (j + 1) * block)
            added = dot(together, w_o1[:, :, :, :, at].reshape(2 * RING * per * hdim, block))
            hid[:, at] = (xs[k, c * RING + j].astype(F32) + added).astype(BF16)
        ri = lax.broadcasted_iota(jnp.int32, (img_tok, rows), 0)
        ci = lax.broadcasted_iota(jnp.int32, (img_tok, rows), 1)
        take = (ci == ri + metas[k, 1:2, :]).astype(F32).astype(BF16)
        total = jnp.zeros(part.shape, F32)
        for j in range(RING):
            at = slice(j * block, (j + 1) * block)
            total = total + dot(dot(take, hid[:, at]).astype(BF16), up1[at, :])
        part[...] = total
        tail_copy(0).start()
        tail_copy(0).wait_recv()
        value = part[...] + got[...] + skip[...].astype(F32)
        upper[...] = (value / (1.0 + jnp.exp(-value))).astype(BF16)
        present = metas[k, 2:3, :img_tok] > 0
        weighted = jnp.where(present, cots[...].astype(F32), 0.0).astype(BF16)
        pair[0] = dot(weighted, upper[...])
        tail_copy(2).start()
        guess = lax.dot_general(ups[...], upper[...], (((1,), (1,)), ((), ())), preferred_element_type=F32)
        p_own[...] = jnp.where(present, guess, 0.0).astype(BF16)
        send_result(0)
        tail_copy(2).wait()
        ys[y] = pair[0] + pair[1]
        for n in (3, 4, 5):
            tail_copy(n).start()
        for n in (3, 4, 5):
            tail_copy(n).wait()
        zs[z] = ys[0] + ys[1] + ys[2] + ys[3]
        for n in (6, 7, 8):
            tail_copy(n).start()
        for n in (6, 7, 8):
            tail_copy(n).wait()
        g_own[...] = zs[0] + zs[1] + zs[2] + zs[3]
        send_result(1)
        tail_copy(0).wait_send()

    for j in (1, 2, 3):
        scatter_q(j).wait_send()

    @section_zero
    def _():
        for j in (1, 2, 3):
            scatter_o(j).wait_send()

        @pl.when(c == 0)
        def _():
            give(7).wait_send()
            give(8).wait_send()

    @section_one
    def _():
        whole_o().wait_send()
        o1.drain()

    g_cp.wait_send()
    m_cp.wait_send()
    for g in (q0, o0, q1):
        g.drain()
    for r in h_ring[1] + x_ring:
        r.drain()

    @pl.when((s == 1) & (c == 1))
    def _():
        pred[...] = p_own[...]
        grad[...] = g_own[...]
        result_copy(0, None).wait_send()
        result_copy(1, None).wait_send()

    @pl.when((s == 0) | (c == 0))
    def _():
        result_copy(0, None).wait_recv()
        result_copy(1, None).wait_recv()
        pred[...] = p_in[...]
        grad[...] = g_in[...]

    @pl.when((s == 1) & (c == 0))
    def _():
        for n in (0, 1):
            for core in (0, 1):
                result_copy(n, core).wait_send()


def window(wq, wo, tokens, patches_t, wd1, wd2, wu1, wu2_t, gain, segment, start, count, cot_t):
    rows, width = tokens.shape
    block = width // RING
    depth, wide_q = wq.shape[1:]
    depth_o = wo.shape[0]
    img_tok = patches_t.shape[1]
    channels = wd1.shape[1]
    pix = wu2_t.shape[0]
    head_cols = wide_q // 3
    dma = pltpu.SemaphoreType.DMA
    vm = pltpu.VMEM
    scratch = [
        vm((2, RING, RING, 2, depth, wide_q), BF16),
        vm((RING, RING, 2, depth_o, block), BF16),
        vm((RING, RING, 2, depth_o, width), BF16),
        vm((2, 2 * RING, rows, block), BF16),
        vm((2, 2 * RING, rows, head_cols), BF16),
        vm((2, rows, wide_q), F32),
        vm((2, rows, wide_q), BF16),
        vm((2, rows, rows), F32),
        vm((2, rows, 1), F32),
        vm((2,) + gain.shape, F32),
        vm((2, 8, rows), jnp.int32),
        vm((img_tok, channels), BF16),
        vm(wd2.shape, BF16),
        vm(wu1.shape, BF16),
        vm((img_tok, channels), F32),
        vm((img_tok, channels), F32),
        vm((img_tok, channels), BF16),
        vm(cot_t.shape, BF16),
        vm(wu2_t.shape, BF16),
        vm((pix, img_tok), BF16),
        vm((pix, img_tok), BF16),
        vm((pix, channels), F32),
        vm((pix, channels), F32),
        vm((2, pix, channels), F32),
        vm((RING, pix, channels), F32),
        vm((RING, pix, channels), F32),
        dma((4,)), dma((4,)), dma((4,)), dma((2,)), dma((1,)), dma((2,)),
        dma((4, 2, 4)), dma((4, 2, 4)), dma((4, 2, 4)), dma((4, 2, 4)),
        dma((3, 2, 8)), dma((3, 2, 8)), dma((9,)), dma((9,)), dma((13,)), dma((11,)), dma((4,)),
    ]
    sm = pl.BlockSpec(memory_space=pltpu.SMEM)
    return pl.pallas_call(
        kernel,
        out_shape=(
            jax.ShapeDtypeStruct((rows, width), BF16),
            jax.ShapeDtypeStruct((pix, img_tok), BF16),
            jax.ShapeDtypeStruct((pix, channels), F32),
        ),
        in_specs=[ANY, ANY, ANY, VM, VM, ANY, ANY, VM, ANY, VM, sm, sm, VM],
        out_specs=(VM, VM, VM),
        scratch_shapes=scratch,
        compiler_params=pltpu.CompilerParams(collective_id=0, has_side_effects=True,
                                             vmem_limit_bytes=63 << 20),
        name="window",
    )(wq, wo, tokens, patches_t, wd1, wd2, wu1, wu2_t, gain, segment, start, count, cot_t)


def shards(
    tokens_in, patches, segment_ids, img_start, img_count, norm_gain, w_qkv, w_out, w_down1, w_down2,
    w_up1, w_up2, cotangent,
):
    rows, width = tokens_in.shape[1:]
    depth, heads, three, hdim = w_qkv.shape[1:]
    wide_q = heads // RING * three * hdim
    block = width // RING
    wq = jnp.transpose(w_qkv[0].reshape(depth, RING, wide_q), (1, 0, 2))
    gain = norm_gain.reshape(2 * RING, 1, block)
    hidden, pred, grad = window(wq, w_out[0], tokens_in[0], patches[0].T, w_down1, w_down2, w_up1,
                                w_up2.T, gain, segment_ids, img_start, img_count, cotangent[0].T)
    return (hidden[None, None], pred.T[None], grad.T)


def solution(mesh):
    placed = (
        P("dp", None, "tp"),
        P("dp", None, None),
        P("dp", None),
        P("dp"),
        P("dp"),
        P("section", None),
        P("section", "dp", "tp", None, None),
        P("section", "dp", "tp"),
        P(),
        P(None, "tp"),
        P("tp", None),
        P(None, "section"),
        P("dp", None, "section"),
    )
    return jax.shard_map(
        shards,
        mesh=mesh,
        in_specs=placed,
        out_specs=(P("section", "dp", None, "tp"), P("dp", None, "section"), P(None, "section")),
        check_vma=False,
    )
```

```python
import math

import jax
import jax.numpy as jnp
from jax import lax
from jax.experimental import pallas as pl
from jax.experimental.pallas import tpu as pltpu
from jax.sharding import PartitionSpec as P

EPSILON = 1e-05
MESH = pl.DeviceIdType.MESH
ANY = pl.BlockSpec(memory_space=pl.ANY)
VM = pl.BlockSpec(memory_space=pltpu.VMEM)
RING = 4
BF16, F32 = jnp.bfloat16, jnp.float32


def dot(a, b):
    return jnp.dot(a, b, preferred_element_type=F32)


def outer(a, b):
    return lax.dot_general(a, b, (((0,), (0,)), ((), ())), preferred_element_type=F32)


class Place:
    def __init__(self):
        self.s = lax.axis_index("section")
        self.c = lax.axis_index("tp")
        d = lax.axis_index("dp")
        self.k = lax.rem(d, 2)
        self.y = lax.rem(lax.div(d, 2), RING)
        self.z = lax.div(d, 2 * RING)
        self.x = 2 * self.s + self.k

    def at(self, dx=0, dy=0, dz=0, sibling=False):
        x = lax.rem(self.x + dx, RING)
        y = lax.rem(self.y + dy, RING)
        z = lax.rem(self.z + dz, RING)
        return {
            "section": lax.div(x, 2),
            "tp": 1 - self.c if sibling else self.c,
            "dp": z * 8 + y * 2 + lax.rem(x, 2),
        }

    def partner(self):
        return {"section": self.s, "tp": self.c, "dp": self.z * 8 + self.y * 2 + 1 - self.k}


def remote(src, dst, send, recv, peer):
    return pltpu.make_async_remote_copy(
        src_ref=src, dst_ref=dst, send_sem=send, recv_sem=recv, device_id=peer, device_id_type=MESH
    )


class Spread:
    def __init__(self, me, ref, s1, r1, s2, r2):
        self.me, self.ref, self.sems = me, ref, (s1, r1, s2, r2)

    def first(self, kk, n):
        me, ref = self.me, self.ref
        s1, r1 = self.sems[:2]
        step = 1 if n % 2 == 0 else 3
        peer = me.at(dy=step) if kk == 0 else me.at(dz=step)
        if n < 2:
            part = ref.at[me.z, me.y, kk]
        else:
            back = 4 - step
            zz = me.z if kk == 0 else lax.rem(me.z + back, RING)
            yy = lax.rem(me.y + back, RING) if kk == 0 else me.y
            half = ref.shape[3] // 2
            part = ref.at[zz, yy, kk, pl.ds((n - 2) * half, half)]
        return remote(part, part, s1.at[kk, n], r1.at[kk, n], peer)

    def second(self, kk, n):
        me, ref = self.me, self.ref
        s2, r2 = self.sems[2:]
        step = 1 if n % 2 == 0 else 3
        peer = me.at(dz=step) if kk == 0 else me.at(dy=step)
        if n < 2:
            part = ref.at[me.z, :, kk] if kk == 0 else ref.at[:, me.y, kk]
        else:
            piece = pl.ds(2 * (n - 2), 2)
            back = 4 - step
            if kk == 0:
                part = ref.at[lax.rem(me.z + back, RING), piece, kk]
            else:
                part = ref.at[piece, lax.rem(me.y + back, RING), kk]
        return remote(part, part, s2.at[kk, n], r2.at[kk, n], peer)

    def own1(self):
        for kk in (0, 1):
            for n in (0, 1):
                self.first(kk, n).start()

    def pass1(self):
        for kk in (0, 1):
            for n in (0, 1):
                self.first(kk, n).wait_recv()
                self.first(kk, n + 2).start()

    def own2(self):
        for kk in (0, 1):
            for n in (2, 3):
                self.first(kk, n).wait_recv()
            for n in (0, 1):
                self.second(kk, n).start()

    def pass2(self):
        for kk in (0, 1):
            for n in (0, 1):
                self.second(kk, n).wait_recv()
                self.second(kk, n + 2).start()

    def done(self):
        for kk in (0, 1):
            for n in (2, 3):
                self.second(kk, n).wait_recv()

    def drain(self):
        for kk in (0, 1):
            for n in range(4):
                self.first(kk, n).wait_send()
                self.second(kk, n).wait_send()


class Ring:
    def __init__(self, me, ref, ss, rs):
        self.me, self.ref, self.ss, self.rs = me, ref, ss, rs

    def copy(self, n):
        me, ref = self.me, self.ref
        half = ref.shape[1] // 2

        def block(back):
            return me.c * RING + lax.rem(me.x + back, RING)

        up, down, side = me.at(dx=1), me.at(dx=3), me.at(sibling=True)
        part, peer = (
            lambda: (ref.at[block(0)], up),
            lambda: (ref.at[block(0)], down),
            lambda: (ref.at[block(0)], side),
            lambda: (ref.at[block(3), pl.ds(0, half)], up),
            lambda: (ref.at[block(1), pl.ds(half, half)], down),
            lambda: (ref.at[block(3)], side),
            lambda: (ref.at[block(1)], side),
            lambda: (ref.at[block(2)], side),
        )[n]()
        return remote(part, part, self.ss.at[n], self.rs.at[n], peer)

    def start(self):
        for n in (0, 1, 2):
            self.copy(n).start()

    def direct(self):
        self.copy(0).wait_recv()
        self.copy(3).start()
        self.copy(5).start()
        self.copy(1).wait_recv()
        self.copy(4).start()
        self.copy(6).start()

    def far(self):
        self.copy(3).wait_recv()
        self.copy(4).wait_recv()
        self.copy(7).start()

    def finish(self):
        for n in (2, 5, 6, 7):
            self.copy(n).wait_recv()

    def drain(self):
        for n in range(8):
            self.copy(n).wait_send()


def kernel(
    wq, wo, tokens, patches_t, wd1, wd2, wu1, wu2_t, gain, segment, start_in, count_in, cot_t,
    hid, pred, grad,
    w_q, w_o0, w_o1, xs, heads, acc, qkv, bias, ssq, gains, metas, skip, down2, up1,
    part, got, upper, cots, ups, p_own, p_in, g_own, g_in, pair, ys, zs,
    s0q, r0q, s0o, r0o, s0w, r0w, s1, r1, s2, r2, ring_s, ring_r, sx, rx, st, rt, loc,
):
    me = Place()
    s, c, k, x, y, z = me.s, me.c, me.k, me.x, me.y, me.z
    rows = tokens.shape[0]
    img_tok = patches_t.shape[1]
    block = xs.shape[3]
    mine = c * RING + x
    side = me.at(sibling=True)

    loads = [
        pltpu.make_async_copy(tokens, hid, loc.at[0]),
        pltpu.make_async_copy(wd2, down2, loc.at[1]),
        pltpu.make_async_copy(wu1, up1, loc.at[2]),
        pltpu.make_async_copy(gain, gains.at[s], loc.at[3]),
    ]
    for cp in loads:
        cp.start()
    metas[k, 0:1, :] = segment[...]
    metas[k, 1:2, :] = jnp.full((1, rows), start_in[0], jnp.int32)
    metas[k, 2:3, :] = jnp.full((1, rows), count_in[0], jnp.int32)
    metas[k, 3:8, :] = jnp.zeros((5, rows), jnp.int32)

    peers = ([me.at(dx=j) for j in (1, 2, 3)] + [me.at(dy=j) for j in (1, 2, 3)]
             + [me.at(dz=j) for j in (1, 2, 3)] + [side])
    across = dict(me.at(dx=2), tp=1 - c)
    barrier = pltpu.get_barrier_semaphore()
    for peer in peers + [across]:
        pl.semaphore_signal(barrier, inc=1, device_id=peer, device_id_type=MESH)
    pl.semaphore_wait(barrier, len(peers) + 1)

    depth = wq.shape[1]
    waves = [pl.ds(w * depth // 2, depth // 2) for w in (0, 1)]

    def scatter_q(j, w):
        return remote(wq.at[lax.rem(x + j, RING), waves[w]], w_q.at[s, z, y, k, waves[w]], s0q.at[w, j],
                      r0q.at[w, x], me.at(dx=j))

    def scatter_o(j):
        cols = pl.ds(pl.multiple_of(lax.rem(x + j, RING) * block, block), block)
        return remote(wo.at[:, cols], w_o0.at[z, y, k], s0o.at[j], r0o.at[k], me.at(dx=j))

    def whole_o():
        return remote(wo, w_o1.at[z, y, k], s0w.at[0], r0w.at[k], me.partner())

    def start_q():
        for w in (0, 1):
            for j in (1, 3, 2):
                scatter_q(j, w).start()
            pltpu.make_async_copy(wq.at[x, waves[w]], w_q.at[s, z, y, k, waves[w]], r0q.at[w, x]).start()

    def start_o():
        for j in (1, 3, 2):
            scatter_o(j).start()
        own_cols = pl.ds(pl.multiple_of(x * block, block), block)
        pltpu.make_async_copy(wo.at[:, own_cols], w_o0.at[z, y, k], r0o.at[k]).start()

    def start_w():
        whole_o().start()
        pltpu.make_async_copy(wo, w_o1.at[z, y, k], r0w.at[k]).start()

    section_zero, section_one = pl.when(s == 0), pl.when(s == 1)
    section_zero(start_q)

    for cp in loads:
        cp.wait()
    g_cp = remote(gains.at[s], gains.at[s], sx.at[3], rx.at[3], me.at(dx=2))
    m_cp = remote(metas.at[k], metas.at[k], sx.at[4], rx.at[4], me.at(dx=1))
    g_cp.start()
    m_cp.start()

    def give(n):
        src, dst = ((cot_t, cots), (wu2_t, ups))[n - 7]
        return remote(src, dst, sx.at[n], rx.at[n], me.at(dx=2))

    @pl.when((s == 0) & (c == 0))
    def _():
        give(7).start()
        give(8).start()

    @pl.when((s == 1) & (c == 1))
    def _():
        cots[...] = cot_t[...]
        ups[...] = wu2_t[...]

    inner = outer(patches_t[...], wd1[...])
    skip[...] = (inner / (1.0 + jnp.exp(-inner))).astype(BF16)
    own_start, own_count = metas[k, 1:2, :], metas[k, 2:3, :]
    rr = lax.broadcasted_iota(jnp.int32, (rows, img_tok), 0)
    ii = lax.broadcasted_iota(jnp.int32, (rows, img_tok), 1)
    put = (rr == ii + own_start[:, :img_tok]).astype(F32).astype(BF16)
    rb = lax.broadcasted_iota(jnp.int32, (rows, block), 0)
    here = (rb >= own_start) & (rb < own_start + img_tok) & (own_count > 0)
    for j in range(RING):
        image = dot(skip[...], down2[:, j * block:(j + 1) * block]).astype(BF16)
        moved = dot(put, image)
        old = hid[:, j * block:(j + 1) * block].astype(F32)
        xs[k, c * RING + j] = jnp.where(here, moved, old).astype(BF16)

    own = pl.ds(c * RING, RING)
    low, high = pl.ds(0, rows // 2), pl.ds(rows // 2, rows // 2)

    def x0_copy(n):
        if n == 0:
            what, peer = xs.at[k, own, low], me.at(dx=1)
        elif n == 1:
            what, peer = xs.at[k, own, high], me.at(dx=3)
        elif n == 2:
            what, peer = xs.at[k, own], side
        elif n == 5:
            what, peer = xs.at[1 - k, own, low], side
        else:
            what, peer = xs.at[1 - k, own, high], side
        return remote(what, what, sx.at[n], rx.at[n], peer)

    refs = [w_q.at[0, :, :, :, waves[0]], w_q.at[0, :, :, :, waves[1]], w_o0, w_q.at[1], w_o1]
    q0a, q0b, o0, q1, o1 = [Spread(me, ref, s1.at[i], r1.at[i], s2.at[i], r2.at[i])
                            for i, ref in enumerate(refs)]

    def landed(ref, sem):
        pltpu.make_async_copy(ref, ref, sem).wait()

    def mask_of(m):
        segment, start, count = metas[m, 0:1, :], metas[m, 1:2, :], metas[m, 2:3, :]
        one_hot = (lax.broadcasted_iota(jnp.int32, (8, rows), 0) == segment).astype(F32).astype(BF16)
        same = outer(one_hot, one_hot)
        i = lax.broadcasted_iota(jnp.int32, (rows, rows), 0)
        j = lax.broadcasted_iota(jnp.int32, (rows, rows), 1)
        in_i = (i >= start) & (i < start + img_tok) & (count > 0)
        in_j = (j >= start) & (j < start + img_tok)
        ok = (same > 0.5) & ((j <= i) | (in_i & in_j))
        bias[m] = jnp.where(ok, 0.0, -1e30)

    for w, spread in enumerate((q0a, q0b)):
        for kk in (0, 1):
            landed(w_q.at[0, z, y, kk, waves[w]], r0q.at[w, kk])
        spread.own1()
    for n in (0, 1, 2):
        x0_copy(n).start()
    section_zero(start_o)
    q0a.pass1()
    q0b.pass1()
    q0a.own2()
    q0b.own2()
    m_cp.wait_recv()
    g_cp.wait_recv()
    mask_of(0)
    mask_of(1)
    x0_copy(0).wait_recv()
    x0_copy(5).start()
    x0_copy(1).wait_recv()
    x0_copy(6).start()

    @section_one
    def _():
        start_q()
        start_w()

    q0a.pass2()
    q0b.pass2()
    for kk in (0, 1):
        landed(w_o0.at[z, y, kk], r0o.at[kk])
    o0.own1()
    for n in (2, 5, 6):
        x0_copy(n).wait_recv()

    def band(m, step, first=False):
        pieces, squares = [], 0.0
        zz, yy = lax.rem(z + step, RING), lax.rem(y + step, RING)

        def take(b, at):
            values = xs[m, b, :, at].astype(F32)
            pieces.append((values * gains[0, b, :, at]).astype(BF16))
            return jnp.sum(values * values, axis=1, keepdims=True)

        half = block // 2
        depth = half // 2
        for b in (0, 1):
            for at in (0, half):
                squares += take(2 * zz + b, slice(at, at + depth))
        for b in range(RING):
            at = pl.ds(pl.multiple_of(lax.rem(yy, 2) * half + depth, depth), depth)
            squares += take(2 * b + lax.div(yy, 2), at)
        weights = jnp.concatenate(
            [w_q[0, zz, :, 0].reshape(block, acc.shape[2]), w_q[0, :, yy, 1].reshape(block, acc.shape[2])], axis=0)
        total = dot(jnp.concatenate(pieces, axis=1), weights)
        if first:
            acc[m] = total
            ssq[m] = squares
        else:
            acc[m] += total
            ssq[m] += squares

    def scaled(m):
        scale = lax.rsqrt(ssq[m] * (1.0 / (2 * RING * block)) + EPSILON)
        qkv[m] = (acc[m] * scale).astype(BF16)

    halves = [pl.ds(r * rows // 2, rows // 2) for r in (0, 1)]

    def project1(m, r):
        at = halves[r]
        squares, total = 0.0, 0.0
        for b in range(0, 2 * RING, 2):
            pieces = []
            for n in (b, b + 1):
                values = xs[m, n, at].astype(F32)
                squares += jnp.sum(values * values, axis=1, keepdims=True)
                pieces.append((values * gains[1, n]).astype(BF16))
            total += dot(jnp.concatenate(pieces, axis=1), w_q[1, b // 2].reshape(2 * block, acc.shape[2]))
        scale = lax.rsqrt(squares * (1.0 / (2 * RING * block)) + EPSILON)
        qkv[m, at] = (total * scale).astype(BF16)

    hdim = 128
    per = heads.shape[3] // hdim
    q_rows = 128

    def attend(m, r):
        for i in range(r * rows // (2 * q_rows), (r + 1) * rows // (2 * q_rows)):
            at = pl.ds(i * q_rows, q_rows)
            for h in range(per):
                base = 3 * h * hdim
                query = qkv[m, at, base:base + hdim]
                keys = qkv[m, :, base + hdim:base + 2 * hdim]
                vals = qkv[m, :, base + 2 * hdim:base + 3 * hdim]
                scores = lax.dot_general(query, keys, (((1,), (1,)), ((), ())), preferred_element_type=F32)
                scores = scores * (1.0 / math.sqrt(hdim)) + bias[m, at, :]
                probs = jnp.exp(scores - jnp.max(scores, axis=1, keepdims=True))
                probs = (probs * (1.0 / jnp.sum(probs, axis=1, keepdims=True))).astype(BF16)
                heads[m, mine, at, h * hdim:(h + 1) * hdim] = dot(probs, vals).astype(BF16)

    units = [(m, r) for m in (0, 1) for r in (0, 1)]
    h0, h1 = [[Ring(me, heads.at[m, :, halves[r]], ring_s.at[n, m, r], ring_r.at[n, m, r]) for m, r in units]
              for n in (0, 1)]
    xr = [Ring(me, xs.at[m, :, halves[r]], ring_s.at[2, m, r], ring_r.at[2, m, r]) for m, r in units]

    def mix0(m, r):
        at = halves[r]
        together = jnp.concatenate([heads[m, b, at] for b in range(2 * RING)], axis=1)
        added = dot(together, w_o0[...].reshape(2 * RING * per * hdim, block))
        xs[m, mine, at] = (xs[m, mine, at].astype(F32) + added).astype(BF16)

    def mixed(u):
        h0[u].finish()
        mix0(*units[u])
        h0[u].drain()
        xr[u].start()

    def attended(ring, u):
        attend(*units[u])
        ring[u].start()

    o0.pass1()
    for kk in (0, 1):
        landed(w_q.at[1, z, y, kk, waves[0]], r0q.at[0, 2 + kk])
        landed(w_q.at[1, z, y, kk, waves[1]], r0q.at[1, 2 + kk])
    q1.own1()
    for step in (0, 1, 3):
        for m in (0, 1):
            band(m, step, step == 0)
    for n in (0, 1, 2, 5, 6):
        x0_copy(n).wait_send()
    q0a.done()
    q0b.done()
    o0.own2()
    band(0, 2)
    scaled(0)
    attended(h0, 0)
    q1.pass1()

    @section_one
    def _():
        for kk in (0, 1):
            landed(w_o1.at[z, y, kk], r0w.at[kk])
        o1.own1()

    attended(h0, 1)
    q1.own2()
    band(1, 2)
    scaled(1)
    h0[0].direct()
    attended(h0, 2)
    o0.pass2()
    section_one(o1.pass1)
    h0[0].far()
    h0[1].direct()
    attended(h0, 3)
    o0.done()
    mixed(0)
    h0[1].far()
    h0[2].direct()
    mixed(1)
    h0[2].far()
    h0[3].direct()
    q1.pass2()
    section_one(o1.own2)
    mixed(2)
    xr[0].direct()
    h0[3].far()
    mixed(3)
    xr[0].far()
    xr[1].direct()
    xr[0].finish()
    q1.done()
    project1(0, 0)
    xr[1].far()
    xr[2].direct()
    xr[1].finish()
    project1(0, 1)
    section_one(o1.pass2)
    attended(h1, 0)
    xr[2].far()
    xr[3].direct()
    attended(h1, 1)
    xr[2].finish()
    project1(1, 0)
    xr[3].far()
    h1[0].direct()
    xr[3].finish()
    project1(1, 1)
    h1[0].far()
    h1[1].direct()
    attended(h1, 2)
    h1[1].far()
    attended(h1, 3)

    @section_zero
    def _():
        for j in range(RING):
            hid[:, j * block:(j + 1) * block] = xs[k, c * RING + j]

    h1[2].direct()
    h1[2].far()
    h1[3].direct()

    def mix1(r):
        at = halves[r]
        together = jnp.concatenate([heads[k, b, at] for b in range(2 * RING)], axis=1)
        for j in range(RING):
            cols = slice(j * block, (j + 1) * block)
            added = dot(together, w_o1[:, :, :, :, cols].reshape(2 * RING * per * hdim, block))
            hid[at, cols] = (xs[k, c * RING + j, at].astype(F32) + added).astype(BF16)

    for u in (0, 1, 2):
        h1[u].finish()

    @section_one
    def _():
        o1.done()
        mix1(0)

    h1[3].far()
    h1[3].finish()

    def tail_copy(n):
        if n == 0:
            return remote(part, got, st.at[0], rt.at[0], side)
        if n == 2:
            return remote(pair.at[0], pair.at[1], st.at[2], rt.at[2], me.partner())
        if n < 6:
            return remote(ys.at[y], ys.at[y], st.at[n], rt.at[n], me.at(dy=n - 2))
        return remote(zs.at[z], zs.at[z], st.at[n], rt.at[n], me.at(dz=n - 5))

    def result_copy(n, core):
        src, dst = ((p_own, p_in), (g_own, g_in))[n]
        peer = side if core is None else dict(me.at(dx=2), tp=core)
        index = 0 if core is None else core
        return remote(src, dst, st.at[9 + 2 * n + index], rt.at[9 + n], peer)

    def send_result(n):
        @pl.when(c == 0)
        def _():
            result_copy(n, 0).start()
            result_copy(n, 1).start()

        @pl.when(c == 1)
        def _():
            result_copy(n, None).start()

    @section_one
    def _():
        @pl.when(c == 0)
        def _():
            give(7).wait_recv()
            give(8).wait_recv()

        mix1(1)
        ri = lax.broadcasted_iota(jnp.int32, (img_tok, rows), 0)
        ci = lax.broadcasted_iota(jnp.int32, (img_tok, rows), 1)
        take = (ci == ri + metas[k, 1:2, :]).astype(F32).astype(BF16)
        total = jnp.zeros(part.shape, F32)
        for j in range(RING):
            at = slice(j * block, (j + 1) * block)
            total = total + dot(dot(take, hid[:, at]).astype(BF16), up1[at, :])
        part[...] = total
        tail_copy(0).start()
        tail_copy(0).wait_recv()
        value = part[...] + got[...] + skip[...].astype(F32)
        upper[...] = (value / (1.0 + jnp.exp(-value))).astype(BF16)
        present = metas[k, 2:3, :img_tok] > 0
        weighted = jnp.where(present, cots[...].astype(F32), 0.0).astype(BF16)
        pair[0] = dot(weighted, upper[...])
        tail_copy(2).start()
        guess = lax.dot_general(ups[...], upper[...], (((1,), (1,)), ((), ())), preferred_element_type=F32)
        p_own[...] = jnp.where(present, guess, 0.0).astype(BF16)
        send_result(0)
        tail_copy(2).wait()
        ys[y] = pair[0] + pair[1]
        for n in (3, 4, 5):
            tail_copy(n).start()
        for n in (3, 4, 5):
            tail_copy(n).wait()
        zs[z] = ys[0] + ys[1] + ys[2] + ys[3]
        for n in (6, 7, 8):
            tail_copy(n).start()
        for n in (6, 7, 8):
            tail_copy(n).wait()
        g_own[...] = zs[0] + zs[1] + zs[2] + zs[3]
        send_result(1)
        tail_copy(0).wait_send()

    for j in (1, 2, 3):
        for w in (0, 1):
            scatter_q(j, w).wait_send()

    @section_zero
    def _():
        for j in (1, 2, 3):
            scatter_o(j).wait_send()

        @pl.when(c == 0)
        def _():
            give(7).wait_send()
            give(8).wait_send()

    @section_one
    def _():
        whole_o().wait_send()
        o1.drain()

    g_cp.wait_send()
    m_cp.wait_send()
    for g in (q0a, q0b, o0, q1):
        g.drain()
    for r in h1 + xr:
        r.drain()

    @pl.when((s == 1) & (c == 1))
    def _():
        pred[...] = p_own[...]
        grad[...] = g_own[...]
        result_copy(0, None).wait_send()
        result_copy(1, None).wait_send()

    @pl.when((s == 0) | (c == 0))
    def _():
        result_copy(0, None).wait_recv()
        result_copy(1, None).wait_recv()
        pred[...] = p_in[...]
        grad[...] = g_in[...]

    @pl.when((s == 1) & (c == 0))
    def _():
        for n in (0, 1):
            for core in (0, 1):
                result_copy(n, core).wait_send()


def window(wq, wo, tokens, patches_t, wd1, wd2, wu1, wu2_t, gain, segment, start, count, cot_t):
    rows, width = tokens.shape
    block = width // RING
    depth, wide_q = wq.shape[1:]
    depth_o = wo.shape[0]
    img_tok = patches_t.shape[1]
    channels = wd1.shape[1]
    pix = wu2_t.shape[0]
    head_cols = wide_q // 3
    dma = pltpu.SemaphoreType.DMA
    vm = pltpu.VMEM
    scratch = [
        vm((2, RING, RING, 2, depth, wide_q), BF16),
        vm((RING, RING, 2, depth_o, block), BF16),
        vm((RING, RING, 2, depth_o, width), BF16),
        vm((2, 2 * RING, rows, block), BF16),
        vm((2, 2 * RING, rows, head_cols), BF16),
        vm((2, rows, wide_q), F32),
        vm((2, rows, wide_q), BF16),
        vm((2, rows, rows), F32),
        vm((2, rows, 1), F32),
        vm((2,) + gain.shape, F32),
        vm((2, 8, rows), jnp.int32),
        vm((img_tok, channels), BF16),
        vm(wd2.shape, BF16),
        vm(wu1.shape, BF16),
        vm((img_tok, channels), F32),
        vm((img_tok, channels), F32),
        vm((img_tok, channels), BF16),
        vm(cot_t.shape, BF16),
        vm(wu2_t.shape, BF16),
        vm((pix, img_tok), BF16),
        vm((pix, img_tok), BF16),
        vm((pix, channels), F32),
        vm((pix, channels), F32),
        vm((2, pix, channels), F32),
        vm((RING, pix, channels), F32),
        vm((RING, pix, channels), F32),
        dma((2, 4)), dma((2, 4)), dma((4,)), dma((2,)), dma((1,)), dma((2,)),
        dma((5, 2, 4)), dma((5, 2, 4)), dma((5, 2, 4)), dma((5, 2, 4)),
        dma((3, 2, 2, 8)), dma((3, 2, 2, 8)), dma((9,)), dma((9,)), dma((13,)), dma((11,)), dma((4,)),
    ]
    sm = pl.BlockSpec(memory_space=pltpu.SMEM)
    return pl.pallas_call(
        kernel,
        out_shape=(
            jax.ShapeDtypeStruct((rows, width), BF16),
            jax.ShapeDtypeStruct((pix, img_tok), BF16),
            jax.ShapeDtypeStruct((pix, channels), F32),
        ),
        in_specs=[ANY, ANY, ANY, VM, VM, ANY, ANY, VM, ANY, VM, sm, sm, VM],
        out_specs=(VM, VM, VM),
        scratch_shapes=scratch,
        compiler_params=pltpu.CompilerParams(collective_id=0, has_side_effects=True,
                                             vmem_limit_bytes=63 << 20),
        name="window",
    )(wq, wo, tokens, patches_t, wd1, wd2, wu1, wu2_t, gain, segment, start, count, cot_t)


def shards(
    tokens_in, patches, segment_ids, img_start, img_count, norm_gain, w_qkv, w_out, w_down1, w_down2,
    w_up1, w_up2, cotangent,
):
    rows, width = tokens_in.shape[1:]
    depth, heads, three, hdim = w_qkv.shape[1:]
    wide_q = heads // RING * three * hdim
    block = width // RING
    wq = jnp.transpose(w_qkv[0].reshape(depth, RING, wide_q), (1, 0, 2))
    gain = norm_gain.reshape(2 * RING, 1, block)
    hidden, pred, grad = window(wq, w_out[0], tokens_in[0], patches[0].T, w_down1, w_down2, w_up1,
                                w_up2.T, gain, segment_ids, img_start, img_count, cotangent[0].T)
    return (hidden[None, None], pred.T[None], grad.T)


def solution(mesh):
    placed = (
        P("dp", None, "tp"),
        P("dp", None, None),
        P("dp", None),
        P("dp"),
        P("dp"),
        P("section", None),
        P("section", "dp", "tp", None, None),
        P("section", "dp", "tp"),
        P(),
        P(None, "tp"),
        P("tp", None),
        P(None, "section"),
        P("dp", None, "section"),
    )
    return jax.shard_map(
        shards,
        mesh=mesh,
        in_specs=placed,
        out_specs=(P("section", "dp", None, "tp"), P("dp", None, "section"), P(None, "section")),
        check_vma=False,
    )
```

```python
import math

import jax
import jax.numpy as jnp
from jax import lax
from jax.experimental import pallas as pl
from jax.experimental.pallas import tpu as pltpu
from jax.sharding import PartitionSpec as P

EPSILON = 1e-05
MESH = pl.DeviceIdType.MESH
ANY = pl.BlockSpec(memory_space=pl.ANY)
VM = pl.BlockSpec(memory_space=pltpu.VMEM)
RING = 4
BF16, F32 = jnp.bfloat16, jnp.float32


def dot(a, b):
    return jnp.dot(a, b, preferred_element_type=F32)


def outer(a, b):
    return lax.dot_general(a, b, (((0,), (0,)), ((), ())), preferred_element_type=F32)


class Place:
    def __init__(self):
        self.s = lax.axis_index("section")
        self.c = lax.axis_index("tp")
        d = lax.axis_index("dp")
        self.k = lax.rem(d, 2)
        self.y = lax.rem(lax.div(d, 2), RING)
        self.z = lax.div(d, 2 * RING)
        self.x = 2 * self.s + self.k

    def at(self, dx=0, dy=0, dz=0, sibling=False):
        x = lax.rem(self.x + dx, RING)
        y = lax.rem(self.y + dy, RING)
        z = lax.rem(self.z + dz, RING)
        return {
            "section": lax.div(x, 2),
            "tp": 1 - self.c if sibling else self.c,
            "dp": z * 8 + y * 2 + lax.rem(x, 2),
        }

    def partner(self):
        return {"section": self.s, "tp": self.c, "dp": self.z * 8 + self.y * 2 + 1 - self.k}


def remote(src, dst, send, recv, peer):
    return pltpu.make_async_remote_copy(
        src_ref=src, dst_ref=dst, send_sem=send, recv_sem=recv, device_id=peer, device_id_type=MESH
    )


class Spread:
    def __init__(self, me, ref, s1, r1, s2, r2):
        self.me, self.ref, self.sems = me, ref, (s1, r1, s2, r2)

    def first(self, kk, n):
        me, ref = self.me, self.ref
        s1, r1 = self.sems[:2]
        step = 1 if n % 2 == 0 else 3
        peer = me.at(dy=step) if kk == 0 else me.at(dz=step)
        if n < 2:
            part = ref.at[me.z, me.y, kk]
        else:
            back = 4 - step
            zz = me.z if kk == 0 else lax.rem(me.z + back, RING)
            yy = lax.rem(me.y + back, RING) if kk == 0 else me.y
            half = ref.shape[3] // 2
            part = ref.at[zz, yy, kk, pl.ds((n - 2) * half, half)]
        return remote(part, part, s1.at[kk, n], r1.at[kk, n], peer)

    def second(self, kk, n):
        me, ref = self.me, self.ref
        s2, r2 = self.sems[2:]
        step = 1 if n % 2 == 0 else 3
        peer = me.at(dz=step) if kk == 0 else me.at(dy=step)
        if n < 2:
            part = ref.at[me.z, :, kk] if kk == 0 else ref.at[:, me.y, kk]
        else:
            piece = pl.ds(2 * (n - 2), 2)
            back = 4 - step
            if kk == 0:
                part = ref.at[lax.rem(me.z + back, RING), piece, kk]
            else:
                part = ref.at[piece, lax.rem(me.y + back, RING), kk]
        return remote(part, part, s2.at[kk, n], r2.at[kk, n], peer)

    def own1(self):
        for kk in (0, 1):
            for n in (0, 1):
                self.first(kk, n).start()

    def pass1(self):
        for kk in (0, 1):
            for n in (0, 1):
                self.first(kk, n).wait_recv()
                self.first(kk, n + 2).start()

    def own2(self):
        for kk in (0, 1):
            for n in (2, 3):
                self.first(kk, n).wait_recv()
            for n in (0, 1):
                self.second(kk, n).start()

    def pass2(self):
        for kk in (0, 1):
            for n in (0, 1):
                self.second(kk, n).wait_recv()
                self.second(kk, n + 2).start()

    def done(self):
        for kk in (0, 1):
            for n in (2, 3):
                self.second(kk, n).wait_recv()

    def drain(self):
        for kk in (0, 1):
            for n in range(4):
                self.first(kk, n).wait_send()
                self.second(kk, n).wait_send()


class Ring:
    def __init__(self, me, ref, ss, rs):
        self.me, self.ref, self.ss, self.rs = me, ref, ss, rs

    def copy(self, n):
        me, ref = self.me, self.ref
        half = ref.shape[1] // 2

        def block(back):
            return me.c * RING + lax.rem(me.x + back, RING)

        up, down, side = me.at(dx=1), me.at(dx=3), me.at(sibling=True)
        part, peer = (
            lambda: (ref.at[block(0)], up),
            lambda: (ref.at[block(0)], down),
            lambda: (ref.at[block(0)], side),
            lambda: (ref.at[block(3), pl.ds(0, half)], up),
            lambda: (ref.at[block(1), pl.ds(half, half)], down),
            lambda: (ref.at[block(3)], side),
            lambda: (ref.at[block(1)], side),
            lambda: (ref.at[block(2)], side),
        )[n]()
        return remote(part, part, self.ss.at[n], self.rs.at[n], peer)

    def start(self):
        for n in (0, 1, 2):
            self.copy(n).start()

    def direct(self):
        self.copy(0).wait_recv()
        self.copy(3).start()
        self.copy(5).start()
        self.copy(1).wait_recv()
        self.copy(4).start()
        self.copy(6).start()

    def far(self):
        self.copy(3).wait_recv()
        self.copy(4).wait_recv()
        self.copy(7).start()

    def finish(self):
        for n in (2, 5, 6, 7):
            self.copy(n).wait_recv()

    def drain(self):
        for n in range(8):
            self.copy(n).wait_send()


def kernel(
    wq, wo, tokens, patches_t, wd1, wd2, wu1, wu2_t, gain, segment, start_in, count_in, cot_t,
    hid, pred, grad,
    w_q, w_o0, w_o1, xs, heads, acc, qkv, bias, ssq, gains, metas, pats, skip, down2, up1,
    part, got, upper, cots, ups, p_own, p_in, g_own, g_in, pair, ys, zs,
    s0q, r0q, s0o, r0o, s0w, r0w, s1, r1, s2, r2, ring_s, ring_r, sb, rb, sx, rx, st, rt, loc,
):
    me = Place()
    s, c, k, x, y, z = me.s, me.c, me.k, me.x, me.y, me.z
    rows = tokens.shape[0]
    img_tok = patches_t.shape[1]
    block = xs.shape[3]
    mine = c * RING + x
    side = me.at(sibling=True)

    gain_load = pltpu.make_async_copy(gain, gains.at[s], loc.at[0])
    down_load = pltpu.make_async_copy(wd2, down2, loc.at[1])
    up_load = pltpu.make_async_copy(wu1, up1, loc.at[2])
    own_loads = [pltpu.make_async_copy(tokens.at[:, pl.ds(j * block, block)], xs.at[k, c * RING + j], loc.at[3 + j])
                 for j in range(RING)]
    for cp in [gain_load, down_load] + own_loads + [up_load]:
        cp.start()
    pats[k] = patches_t[...]
    metas[k, 0:1, :] = segment[...]
    metas[k, 1:2, :] = jnp.full((1, rows), start_in[0], jnp.int32)
    metas[k, 2:3, :] = jnp.full((1, rows), count_in[0], jnp.int32)
    metas[k, 3:8, :] = jnp.zeros((5, rows), jnp.int32)

    peers = ([me.at(dx=j) for j in (1, 2, 3)] + [me.at(dy=j) for j in (1, 2, 3)]
             + [me.at(dz=j) for j in (1, 2, 3)] + [side])
    across = dict(me.at(dx=2), tp=1 - c)
    barrier = pltpu.get_barrier_semaphore()
    for peer in peers + [across]:
        pl.semaphore_signal(barrier, inc=1, device_id=peer, device_id_type=MESH)
    pl.semaphore_wait(barrier, len(peers) + 1)

    depth = wq.shape[1]
    waves = [pl.ds(w * depth // 2, depth // 2) for w in (0, 1)]

    def scatter_q(j, w):
        return remote(wq.at[lax.rem(x + j, RING), waves[w]], w_q.at[s, z, y, k, waves[w]], s0q.at[w, j],
                      r0q.at[w, x], me.at(dx=j))

    def scatter_o(j):
        cols = pl.ds(pl.multiple_of(lax.rem(x + j, RING) * block, block), block)
        return remote(wo.at[:, cols], w_o0.at[z, y, k], s0o.at[j], r0o.at[k], me.at(dx=j))

    def whole_o():
        return remote(wo, w_o1.at[z, y, k], s0w.at[0], r0w.at[k], me.partner())

    def start_q():
        for w in (0, 1):
            for j in (1, 3, 2):
                scatter_q(j, w).start()
            pltpu.make_async_copy(wq.at[x, waves[w]], w_q.at[s, z, y, k, waves[w]], r0q.at[w, x]).start()

    def start_o():
        for j in (1, 3, 2):
            scatter_o(j).start()
        own_cols = pl.ds(pl.multiple_of(x * block, block), block)
        pltpu.make_async_copy(wo.at[:, own_cols], w_o0.at[z, y, k], r0o.at[k]).start()

    def start_w():
        whole_o().start()
        pltpu.make_async_copy(wo, w_o1.at[z, y, k], r0w.at[k]).start()

    section_zero, section_one = pl.when(s == 0), pl.when(s == 1)
    low, high = pl.ds(0, rows // 2), pl.ds(rows // 2, rows // 2)

    def rows_copy(j, n):
        part, peer = ((low, me.at(dx=1)), (high, me.at(dx=3)))[n]
        return remote(tokens.at[part, pl.ds(j * block, block)], xs.at[k, c * RING + j, part], sb.at[n, j],
                      rb.at[n, j], peer)

    def core_copy(m, j):
        ref = xs.at[m, c * RING + j]
        n = 2 if m is k else 3
        return remote(ref, ref, sb.at[n, j], rb.at[n, j], side)

    p_cp = remote(pats.at[k], pats.at[k], sx.at[0], rx.at[0], me.at(dx=1))
    p_cp.start()
    section_zero(start_q)
    for j in range(RING):
        for n in (0, 1):
            rows_copy(j, n).start()
    gain_load.wait()
    g_cp = remote(gains.at[s], gains.at[s], sx.at[3], rx.at[3], me.at(dx=2))
    m_cp = remote(metas.at[k], metas.at[k], sx.at[4], rx.at[4], me.at(dx=1))
    g_cp.start()
    m_cp.start()

    def give(n):
        src, dst = ((cot_t, cots), (wu2_t, ups))[n - 7]
        return remote(src, dst, sx.at[n], rx.at[n], me.at(dx=2))

    @pl.when((s == 0) & (c == 0))
    def _():
        give(7).start()
        give(8).start()

    @pl.when((s == 1) & (c == 1))
    def _():
        cots[...] = cot_t[...]
        ups[...] = wu2_t[...]

    def down(m):
        inner = outer(pats[m], wd1[...])
        return (inner / (1.0 + jnp.exp(-inner))).astype(BF16)

    def place(m, j, features):
        start, count = metas[m, 1:2, :], metas[m, 2:3, :]
        row = lax.broadcasted_iota(jnp.int32, (rows, img_tok), 0)
        col = lax.broadcasted_iota(jnp.int32, (rows, img_tok), 1)
        put = (row == col + start[:, :img_tok]).astype(F32).astype(BF16)
        row = lax.broadcasted_iota(jnp.int32, (rows, block), 0)
        here = (row >= start) & (row < start + img_tok) & (count > 0)
        image = dot(features, down2[:, j * block:(j + 1) * block]).astype(BF16)
        old = xs[m, c * RING + j].astype(F32)
        xs[m, c * RING + j] = jnp.where(here, dot(put, image), old).astype(BF16)
        core_copy(m, j).start()

    other = 1 - k
    skip[...] = down(k)
    down_load.wait()
    for j in range(RING):
        own_loads[j].wait()
        place(k, j, skip[...])

    refs = [w_q.at[0, :, :, :, waves[0]], w_q.at[0, :, :, :, waves[1]], w_o0, w_q.at[1], w_o1]
    q0a, q0b, o0, q1, o1 = [Spread(me, ref, s1.at[i], r1.at[i], s2.at[i], r2.at[i])
                            for i, ref in enumerate(refs)]

    def landed(ref, sem):
        pltpu.make_async_copy(ref, ref, sem).wait()

    def mask_of(m):
        segment, start, count = metas[m, 0:1, :], metas[m, 1:2, :], metas[m, 2:3, :]
        one_hot = (lax.broadcasted_iota(jnp.int32, (8, rows), 0) == segment).astype(F32).astype(BF16)
        same = outer(one_hot, one_hot)
        i = lax.broadcasted_iota(jnp.int32, (rows, rows), 0)
        j = lax.broadcasted_iota(jnp.int32, (rows, rows), 1)
        in_i = (i >= start) & (i < start + img_tok) & (count > 0)
        in_j = (j >= start) & (j < start + img_tok)
        ok = (same > 0.5) & ((j <= i) | (in_i & in_j))
        bias[m] = jnp.where(ok, 0.0, -1e30)

    def arrive(j):
        for n in (0, 1):
            rows_copy(j, n).wait_recv()
        place(other, j, upper[...])

    def begin(w, spread):
        for kk in (0, 1):
            landed(w_q.at[0, z, y, kk, waves[w]], r0q.at[w, kk])
        spread.own1()

    p_cp.wait_recv()
    m_cp.wait_recv()
    upper[...] = down(other)
    begin(0, q0a)
    arrive(0)
    begin(1, q0b)
    section_zero(start_o)
    arrive(1)
    q0a.pass1()
    q0b.pass1()
    arrive(2)
    q0a.own2()
    q0b.own2()
    arrive(3)

    @section_one
    def _():
        start_q()
        start_w()

    g_cp.wait_recv()
    mask_of(0)
    mask_of(1)
    for j in range(RING):
        core_copy(k, j).wait_recv()
        core_copy(other, j).wait_recv()

    def band(m, step, first=False):
        pieces, squares = [], 0.0
        zz, yy = lax.rem(z + step, RING), lax.rem(y + step, RING)

        def take(b, at):
            values = xs[m, b, :, at].astype(F32)
            pieces.append((values * gains[0, b, :, at]).astype(BF16))
            return jnp.sum(values * values, axis=1, keepdims=True)

        half = block // 2
        depth = half // 2
        for b in (0, 1):
            for at in (0, half):
                squares += take(2 * zz + b, slice(at, at + depth))
        for b in range(RING):
            at = pl.ds(pl.multiple_of(lax.rem(yy, 2) * half + depth, depth), depth)
            squares += take(2 * b + lax.div(yy, 2), at)
        weights = jnp.concatenate(
            [w_q[0, zz, :, 0].reshape(block, acc.shape[2]), w_q[0, :, yy, 1].reshape(block, acc.shape[2])], axis=0)
        total = dot(jnp.concatenate(pieces, axis=1), weights)
        if first:
            acc[m] = total
            ssq[m] = squares
        else:
            acc[m] += total
            ssq[m] += squares

    def scaled(m):
        scale = lax.rsqrt(ssq[m] * (1.0 / (2 * RING * block)) + EPSILON)
        qkv[m] = (acc[m] * scale).astype(BF16)

    halves = [pl.ds(r * rows // 2, rows // 2) for r in (0, 1)]

    def project1(m, r):
        at = halves[r]
        squares, total = 0.0, 0.0
        for b in range(0, 2 * RING, 2):
            pieces = []
            for n in (b, b + 1):
                values = xs[m, n, at].astype(F32)
                squares += jnp.sum(values * values, axis=1, keepdims=True)
                pieces.append((values * gains[1, n]).astype(BF16))
            total += dot(jnp.concatenate(pieces, axis=1), w_q[1, b // 2].reshape(2 * block, acc.shape[2]))
        scale = lax.rsqrt(squares * (1.0 / (2 * RING * block)) + EPSILON)
        qkv[m, at] = (total * scale).astype(BF16)

    hdim = 128
    per = heads.shape[3] // hdim
    q_rows = 128

    def attend(m, r):
        for i in range(r * rows // (2 * q_rows), (r + 1) * rows // (2 * q_rows)):
            at = pl.ds(i * q_rows, q_rows)
            for h in range(per):
                base = 3 * h * hdim
                query = qkv[m, at, base:base + hdim]
                keys = qkv[m, :, base + hdim:base + 2 * hdim]
                vals = qkv[m, :, base + 2 * hdim:base + 3 * hdim]
                scores = lax.dot_general(query, keys, (((1,), (1,)), ((), ())), preferred_element_type=F32)
                scores = scores * (1.0 / math.sqrt(hdim)) + bias[m, at, :]
                probs = jnp.exp(scores - jnp.max(scores, axis=1, keepdims=True))
                probs = (probs * (1.0 / jnp.sum(probs, axis=1, keepdims=True))).astype(BF16)
                heads[m, mine, at, h * hdim:(h + 1) * hdim] = dot(probs, vals).astype(BF16)

    units = [(m, r) for m in (0, 1) for r in (0, 1)]
    h0, h1 = [[Ring(me, heads.at[m, :, halves[r]], ring_s.at[n, m, r], ring_r.at[n, m, r]) for m, r in units]
              for n in (0, 1)]
    xr = [Ring(me, xs.at[m, :, halves[r]], ring_s.at[2, m, r], ring_r.at[2, m, r]) for m, r in units]

    def mix0(m, r):
        at = halves[r]
        together = jnp.concatenate([heads[m, b, at] for b in range(2 * RING)], axis=1)
        added = dot(together, w_o0[...].reshape(2 * RING * per * hdim, block))
        xs[m, mine, at] = (xs[m, mine, at].astype(F32) + added).astype(BF16)

    def mixed(u):
        h0[u].finish()
        mix0(*units[u])
        h0[u].drain()
        xr[u].start()

    def attended(ring, u):
        attend(*units[u])
        ring[u].start()

    for m in (0, 1):
        band(m, 0, True)
    q0a.pass2()
    q0b.pass2()
    for kk in (0, 1):
        landed(w_o0.at[z, y, kk], r0o.at[kk])
    o0.own1()
    for m in (0, 1):
        band(m, 1)
    o0.pass1()
    for kk in (0, 1):
        landed(w_q.at[1, z, y, kk, waves[0]], r0q.at[0, 2 + kk])
        landed(w_q.at[1, z, y, kk, waves[1]], r0q.at[1, 2 + kk])
    q1.own1()
    for m in (0, 1):
        band(m, 3)
    for j in range(RING):
        core_copy(k, j).wait_send()
        core_copy(other, j).wait_send()
    q0a.done()
    q0b.done()
    o0.own2()
    band(0, 2)
    scaled(0)
    attended(h0, 0)
    q1.pass1()

    @section_one
    def _():
        for kk in (0, 1):
            landed(w_o1.at[z, y, kk], r0w.at[kk])
        o1.own1()

    attended(h0, 1)
    q1.own2()
    band(1, 2)
    scaled(1)
    h0[0].direct()
    attended(h0, 2)
    o0.pass2()
    section_one(o1.pass1)
    h0[0].far()
    h0[1].direct()
    attended(h0, 3)
    o0.done()
    mixed(0)
    h0[1].far()
    h0[2].direct()
    mixed(1)
    h0[2].far()
    h0[3].direct()
    q1.pass2()
    section_one(o1.own2)
    mixed(2)
    xr[0].direct()
    h0[3].far()
    mixed(3)
    xr[0].far()
    xr[1].direct()
    xr[0].finish()
    q1.done()
    project1(0, 0)
    xr[1].far()
    xr[2].direct()
    xr[1].finish()
    project1(0, 1)
    section_one(o1.pass2)
    attended(h1, 0)
    xr[2].far()
    xr[3].direct()
    attended(h1, 1)
    xr[2].finish()
    project1(1, 0)
    xr[3].far()
    h1[0].direct()
    xr[3].finish()
    project1(1, 1)
    h1[0].far()
    h1[1].direct()
    attended(h1, 2)
    h1[1].far()
    attended(h1, 3)

    @section_zero
    def _():
        for j in range(RING):
            hid[:, j * block:(j + 1) * block] = xs[k, c * RING + j]

    h1[2].direct()
    h1[2].far()
    h1[3].direct()

    def mix1(r):
        at = halves[r]
        together = jnp.concatenate([heads[k, b, at] for b in range(2 * RING)], axis=1)
        for j in range(RING):
            cols = slice(j * block, (j + 1) * block)
            added = dot(together, w_o1[:, :, :, :, cols].reshape(2 * RING * per * hdim, block))
            hid[at, cols] = (xs[k, c * RING + j, at].astype(F32) + added).astype(BF16)

    for u in (0, 1, 2):
        h1[u].finish()

    @section_one
    def _():
        up_load.wait()
        o1.done()
        mix1(0)

    h1[3].far()
    h1[3].finish()

    def tail_copy(n):
        if n == 0:
            return remote(part, got, st.at[0], rt.at[0], side)
        if n == 2:
            return remote(pair.at[0], pair.at[1], st.at[2], rt.at[2], me.partner())
        if n < 6:
            return remote(ys.at[y], ys.at[y], st.at[n], rt.at[n], me.at(dy=n - 2))
        return remote(zs.at[z], zs.at[z], st.at[n], rt.at[n], me.at(dz=n - 5))

    def result_copy(n, core):
        src, dst = ((p_own, p_in), (g_own, g_in))[n]
        peer = side if core is None else dict(me.at(dx=2), tp=core)
        index = 0 if core is None else core
        return remote(src, dst, st.at[9 + 2 * n + index], rt.at[9 + n], peer)

    def send_result(n):
        @pl.when(c == 0)
        def _():
            result_copy(n, 0).start()
            result_copy(n, 1).start()

        @pl.when(c == 1)
        def _():
            result_copy(n, None).start()

    @section_one
    def _():
        @pl.when(c == 0)
        def _():
            give(7).wait_recv()
            give(8).wait_recv()

        mix1(1)
        ri = lax.broadcasted_iota(jnp.int32, (img_tok, rows), 0)
        ci = lax.broadcasted_iota(jnp.int32, (img_tok, rows), 1)
        take = (ci == ri + metas[k, 1:2, :]).astype(F32).astype(BF16)
        total = jnp.zeros(part.shape, F32)
        for j in range(RING):
            at = slice(j * block, (j + 1) * block)
            total = total + dot(dot(take, hid[:, at]).astype(BF16), up1[at, :])
        part[...] = total
        tail_copy(0).start()
        tail_copy(0).wait_recv()
        value = part[...] + got[...] + skip[...].astype(F32)
        upper[...] = (value / (1.0 + jnp.exp(-value))).astype(BF16)
        present = metas[k, 2:3, :img_tok] > 0
        weighted = jnp.where(present, cots[...].astype(F32), 0.0).astype(BF16)
        pair[0] = dot(weighted, upper[...])
        tail_copy(2).start()
        guess = lax.dot_general(ups[...], upper[...], (((1,), (1,)), ((), ())), preferred_element_type=F32)
        p_own[...] = jnp.where(present, guess, 0.0).astype(BF16)
        send_result(0)
        tail_copy(2).wait()
        ys[y] = pair[0] + pair[1]
        for n in (3, 4, 5):
            tail_copy(n).start()
        for n in (3, 4, 5):
            tail_copy(n).wait()
        zs[z] = ys[0] + ys[1] + ys[2] + ys[3]
        for n in (6, 7, 8):
            tail_copy(n).start()
        for n in (6, 7, 8):
            tail_copy(n).wait()
        g_own[...] = zs[0] + zs[1] + zs[2] + zs[3]
        send_result(1)
        tail_copy(0).wait_send()

    for j in (1, 2, 3):
        for w in (0, 1):
            scatter_q(j, w).wait_send()

    @section_zero
    def _():
        for j in (1, 2, 3):
            scatter_o(j).wait_send()

        @pl.when(c == 0)
        def _():
            give(7).wait_send()
            give(8).wait_send()

    @section_one
    def _():
        whole_o().wait_send()
        o1.drain()

    section_zero(up_load.wait)
    for j in range(RING):
        for n in (0, 1):
            rows_copy(j, n).wait_send()
    p_cp.wait_send()
    g_cp.wait_send()
    m_cp.wait_send()
    for g in (q0a, q0b, o0, q1):
        g.drain()
    for r in h1 + xr:
        r.drain()

    @pl.when((s == 1) & (c == 1))
    def _():
        pred[...] = p_own[...]
        grad[...] = g_own[...]
        result_copy(0, None).wait_send()
        result_copy(1, None).wait_send()

    @pl.when((s == 0) | (c == 0))
    def _():
        result_copy(0, None).wait_recv()
        result_copy(1, None).wait_recv()
        pred[...] = p_in[...]
        grad[...] = g_in[...]

    @pl.when((s == 1) & (c == 0))
    def _():
        for n in (0, 1):
            for core in (0, 1):
                result_copy(n, core).wait_send()


def window(wq, wo, tokens, patches_t, wd1, wd2, wu1, wu2_t, gain, segment, start, count, cot_t):
    rows, width = tokens.shape
    block = width // RING
    depth, wide_q = wq.shape[1:]
    depth_o = wo.shape[0]
    img_tok = patches_t.shape[1]
    channels = wd1.shape[1]
    pix = wu2_t.shape[0]
    head_cols = wide_q // 3
    dma = pltpu.SemaphoreType.DMA
    vm = pltpu.VMEM
    scratch = [
        vm((2, RING, RING, 2, depth, wide_q), BF16),
        vm((RING, RING, 2, depth_o, block), BF16),
        vm((RING, RING, 2, depth_o, width), BF16),
        vm((2, 2 * RING, rows, block), BF16),
        vm((2, 2 * RING, rows, head_cols), BF16),
        vm((2, rows, wide_q), F32),
        vm((2, rows, wide_q), BF16),
        vm((2, rows, rows), F32),
        vm((2, rows, 1), F32),
        vm((2,) + gain.shape, F32),
        vm((2, 8, rows), jnp.int32),
        vm((2,) + patches_t.shape, BF16),
        vm((img_tok, channels), BF16),
        vm(wd2.shape, BF16),
        vm(wu1.shape, BF16),
        vm((img_tok, channels), F32),
        vm((img_tok, channels), F32),
        vm((img_tok, channels), BF16),
        vm(cot_t.shape, BF16),
        vm(wu2_t.shape, BF16),
        vm((pix, img_tok), BF16),
        vm((pix, img_tok), BF16),
        vm((pix, channels), F32),
        vm((pix, channels), F32),
        vm((2, pix, channels), F32),
        vm((RING, pix, channels), F32),
        vm((RING, pix, channels), F32),
        dma((2, 4)), dma((2, 4)), dma((4,)), dma((2,)), dma((1,)), dma((2,)),
        dma((5, 2, 4)), dma((5, 2, 4)), dma((5, 2, 4)), dma((5, 2, 4)),
        dma((3, 2, 2, 8)), dma((3, 2, 2, 8)), dma((4, 4)), dma((4, 4)), dma((9,)), dma((9,)), dma((13,)), dma((11,)), dma((7,)),
    ]
    sm = pl.BlockSpec(memory_space=pltpu.SMEM)
    return pl.pallas_call(
        kernel,
        out_shape=(
            jax.ShapeDtypeStruct((rows, width), BF16),
            jax.ShapeDtypeStruct((pix, img_tok), BF16),
            jax.ShapeDtypeStruct((pix, channels), F32),
        ),
        in_specs=[ANY, ANY, ANY, VM, VM, ANY, ANY, VM, ANY, VM, sm, sm, VM],
        out_specs=(VM, VM, VM),
        scratch_shapes=scratch,
        compiler_params=pltpu.CompilerParams(collective_id=0, has_side_effects=True,
                                             vmem_limit_bytes=63 << 20),
        name="window",
    )(wq, wo, tokens, patches_t, wd1, wd2, wu1, wu2_t, gain, segment, start, count, cot_t)


def shards(
    tokens_in, patches, segment_ids, img_start, img_count, norm_gain, w_qkv, w_out, w_down1, w_down2,
    w_up1, w_up2, cotangent,
):
    rows, width = tokens_in.shape[1:]
    depth, heads, three, hdim = w_qkv.shape[1:]
    wide_q = heads // RING * three * hdim
    block = width // RING
    wq = jnp.transpose(w_qkv[0].reshape(depth, RING, wide_q), (1, 0, 2))
    gain = norm_gain.reshape(2 * RING, 1, block)
    hidden, pred, grad = window(wq, w_out[0], tokens_in[0], patches[0].T, w_down1, w_down2, w_up1,
                                w_up2.T, gain, segment_ids, img_start, img_count, cotangent[0].T)
    return (hidden[None, None], pred.T[None], grad.T)


def solution(mesh):
    placed = (
        P("dp", None, "tp"),
        P("dp", None, None),
        P("dp", None),
        P("dp"),
        P("dp"),
        P("section", None),
        P("section", "dp", "tp", None, None),
        P("section", "dp", "tp"),
        P(),
        P(None, "tp"),
        P("tp", None),
        P(None, "section"),
        P("dp", None, "section"),
    )
    return jax.shard_map(
        shards,
        mesh=mesh,
        in_specs=placed,
        out_specs=(P("section", "dp", None, "tp"), P("dp", None, "section"), P(None, "section")),
        check_vma=False,
    )
```

```python
import math

import jax
import jax.numpy as jnp
from jax import lax
from jax.experimental import pallas as pl
from jax.experimental.pallas import tpu as pltpu
from jax.sharding import PartitionSpec as P

EPSILON = 1e-05
MESH = pl.DeviceIdType.MESH
ANY = pl.BlockSpec(memory_space=pl.ANY)
VM = pl.BlockSpec(memory_space=pltpu.VMEM)
RING = 4
BF16, F32 = jnp.bfloat16, jnp.float32


def dot(a, b):
    return jnp.dot(a, b, preferred_element_type=F32)


def outer(a, b):
    return lax.dot_general(a, b, (((0,), (0,)), ((), ())), preferred_element_type=F32)


class Place:
    def __init__(self):
        self.s = lax.axis_index("section")
        self.c = lax.axis_index("tp")
        d = lax.axis_index("dp")
        self.k = lax.rem(d, 2)
        self.y = lax.rem(lax.div(d, 2), RING)
        self.z = lax.div(d, 2 * RING)
        self.x = 2 * self.s + self.k

    def at(self, dx=0, dy=0, dz=0, sibling=False):
        x = lax.rem(self.x + dx, RING)
        y = lax.rem(self.y + dy, RING)
        z = lax.rem(self.z + dz, RING)
        return {
            "section": lax.div(x, 2),
            "tp": 1 - self.c if sibling else self.c,
            "dp": z * 8 + y * 2 + lax.rem(x, 2),
        }

    def partner(self):
        return {"section": self.s, "tp": self.c, "dp": self.z * 8 + self.y * 2 + 1 - self.k}


def remote(src, dst, send, recv, peer):
    return pltpu.make_async_remote_copy(
        src_ref=src, dst_ref=dst, send_sem=send, recv_sem=recv, device_id=peer, device_id_type=MESH
    )


class Spread:
    def __init__(self, me, ref, s1, r1, s2, r2):
        self.me, self.ref, self.sems = me, ref, (s1, r1, s2, r2)

    def first(self, kk, n):
        me, ref = self.me, self.ref
        s1, r1 = self.sems[:2]
        step = 1 if n % 2 == 0 else 3
        peer = me.at(dy=step) if kk == 0 else me.at(dz=step)
        if n < 2:
            part = ref.at[me.z, me.y, kk]
        else:
            back = 4 - step
            zz = me.z if kk == 0 else lax.rem(me.z + back, RING)
            yy = lax.rem(me.y + back, RING) if kk == 0 else me.y
            half = ref.shape[3] // 2
            part = ref.at[zz, yy, kk, pl.ds((n - 2) * half, half)]
        return remote(part, part, s1.at[kk, n], r1.at[kk, n], peer)

    def second(self, kk, n):
        me, ref = self.me, self.ref
        s2, r2 = self.sems[2:]
        step = 1 if n % 2 == 0 else 3
        peer = me.at(dz=step) if kk == 0 else me.at(dy=step)
        if n < 2:
            part = ref.at[me.z, :, kk] if kk == 0 else ref.at[:, me.y, kk]
        else:
            piece = pl.ds(2 * (n - 2), 2)
            back = 4 - step
            if kk == 0:
                part = ref.at[lax.rem(me.z + back, RING), piece, kk]
            else:
                part = ref.at[piece, lax.rem(me.y + back, RING), kk]
        return remote(part, part, s2.at[kk, n], r2.at[kk, n], peer)

    def own1(self):
        for kk in (0, 1):
            for n in (0, 1):
                self.first(kk, n).start()

    def pass1(self):
        for kk in (0, 1):
            for n in (0, 1):
                self.first(kk, n).wait_recv()
                self.first(kk, n + 2).start()

    def own2(self):
        for kk in (0, 1):
            for n in (2, 3):
                self.first(kk, n).wait_recv()
            for n in (0, 1):
                self.second(kk, n).start()

    def pass2(self):
        for kk in (0, 1):
            for n in (0, 1):
                self.second(kk, n).wait_recv()
                self.second(kk, n + 2).start()

    def done(self):
        for kk in (0, 1):
            for n in (2, 3):
                self.second(kk, n).wait_recv()

    def drain(self):
        for kk in (0, 1):
            for n in range(4):
                self.first(kk, n).wait_send()
                self.second(kk, n).wait_send()


class Ring:
    def __init__(self, me, ref, ss, rs):
        self.me, self.ref, self.ss, self.rs = me, ref, ss, rs

    def copy(self, n):
        me, ref = self.me, self.ref
        half = ref.shape[1] // 2

        def block(back):
            return me.c * RING + lax.rem(me.x + back, RING)

        up, down, side = me.at(dx=1), me.at(dx=3), me.at(sibling=True)
        part, peer = (
            lambda: (ref.at[block(0)], up),
            lambda: (ref.at[block(0)], down),
            lambda: (ref.at[block(0)], side),
            lambda: (ref.at[block(3), pl.ds(0, half)], up),
            lambda: (ref.at[block(1), pl.ds(half, half)], down),
            lambda: (ref.at[block(3)], side),
            lambda: (ref.at[block(1)], side),
            lambda: (ref.at[block(2)], side),
        )[n]()
        return remote(part, part, self.ss.at[n], self.rs.at[n], peer)

    def start(self):
        for n in (0, 1, 2):
            self.copy(n).start()

    def direct(self):
        self.copy(0).wait_recv()
        self.copy(3).start()
        self.copy(5).start()
        self.copy(1).wait_recv()
        self.copy(4).start()
        self.copy(6).start()

    def far(self):
        self.copy(3).wait_recv()
        self.copy(4).wait_recv()
        self.copy(7).start()

    def finish(self):
        for n in (2, 5, 6, 7):
            self.copy(n).wait_recv()

    def drain(self):
        for n in range(8):
            self.copy(n).wait_send()


def kernel(
    wq, wo, tokens, patches_t, wd1, wd2, wu1, wu2_t, gain, segment, start_in, count_in, cot_t,
    hid, pred, grad,
    w_q, w_o0, w_o1, xs, heads, acc, qkv, bias, ssq, gains, metas, skip, down2, up1,
    part, got, upper, cots, ups, p_own, p_in, g_own, g_in, ys, zs,
    s0q, r0q, s0o, r0o, s0w, r0w, s1, r1, s2, r2, ring_s, ring_r, sx, rx, st, rt, loc,
):
    me = Place()
    s, c, k, x, y, z = me.s, me.c, me.k, me.x, me.y, me.z
    rows = tokens.shape[0]
    img_tok = patches_t.shape[1]
    block = xs.shape[3]
    mine = c * RING + x
    side = me.at(sibling=True)

    loads = [
        pltpu.make_async_copy(tokens, hid, loc.at[0]),
        pltpu.make_async_copy(wd2, down2, loc.at[1]),
        pltpu.make_async_copy(wu1, up1, loc.at[2]),
        pltpu.make_async_copy(gain, gains.at[s], loc.at[3]),
    ]
    for cp in loads:
        cp.start()
    metas[k, 0:1, :] = segment[...]
    metas[k, 1:2, :] = jnp.full((1, rows), start_in[0], jnp.int32)
    metas[k, 2:3, :] = jnp.full((1, rows), count_in[0], jnp.int32)
    metas[k, 3:8, :] = jnp.zeros((5, rows), jnp.int32)

    place = 2 * y + k

    def plane(n):
        return {"section": s, "tp": c, "dp": 8 * z + lax.rem(place + n, 8)}

    peers = ([me.at(dx=j) for j in (1, 2, 3)] + [plane(n) for n in range(1, 8)]
             + [me.at(dz=j) for j in (1, 2, 3)] + [side])
    across = dict(me.at(dx=2), tp=1 - c)
    barrier = pltpu.get_barrier_semaphore()
    for peer in peers + [across]:
        pl.semaphore_signal(barrier, inc=1, device_id=peer, device_id_type=MESH)
    pl.semaphore_wait(barrier, len(peers) + 1)

    depth = wq.shape[1]
    waves = [pl.ds(w * depth // 2, depth // 2) for w in (0, 1)]

    def scatter_q(j, w):
        return remote(wq.at[lax.rem(x + j, RING), waves[w]], w_q.at[s, z, y, k, waves[w]], s0q.at[w, j],
                      r0q.at[w, x], me.at(dx=j))

    def scatter_o(j):
        cols = pl.ds(pl.multiple_of(lax.rem(x + j, RING) * block, block), block)
        return remote(wo.at[:, cols], w_o0.at[z, y, k], s0o.at[j], r0o.at[k], me.at(dx=j))

    def whole_o():
        return remote(wo, w_o1.at[z, y, k], s0w.at[0], r0w.at[k], me.partner())

    def start_q():
        for w in (0, 1):
            for j in (1, 3, 2):
                scatter_q(j, w).start()
            pltpu.make_async_copy(wq.at[x, waves[w]], w_q.at[s, z, y, k, waves[w]], r0q.at[w, x]).start()

    def start_o():
        for j in (1, 3, 2):
            scatter_o(j).start()
        own_cols = pl.ds(pl.multiple_of(x * block, block), block)
        pltpu.make_async_copy(wo.at[:, own_cols], w_o0.at[z, y, k], r0o.at[k]).start()

    def start_w():
        whole_o().start()
        pltpu.make_async_copy(wo, w_o1.at[z, y, k], r0w.at[k]).start()

    section_zero, section_one = pl.when(s == 0), pl.when(s == 1)
    start_q()

    for cp in loads:
        cp.wait()
    g_cp = remote(gains.at[s], gains.at[s], sx.at[3], rx.at[3], me.at(dx=2))
    m_cp = remote(metas.at[k], metas.at[k], sx.at[4], rx.at[4], me.at(dx=1))
    g_cp.start()
    m_cp.start()

    def give(n):
        src, dst = ((cot_t, cots), (wu2_t, ups))[n - 7]
        return remote(src, dst, sx.at[n], rx.at[n], me.at(dx=2))

    @pl.when((s == 0) & (c == 0))
    def _():
        give(7).start()
        give(8).start()

    @pl.when((s == 1) & (c == 1))
    def _():
        cots[...] = cot_t[...]
        ups[...] = wu2_t[...]

    inner = outer(patches_t[...], wd1[...])
    skip[...] = (inner / (1.0 + jnp.exp(-inner))).astype(BF16)
    own_start, own_count = metas[k, 1:2, :], metas[k, 2:3, :]
    rr = lax.broadcasted_iota(jnp.int32, (rows, img_tok), 0)
    ii = lax.broadcasted_iota(jnp.int32, (rows, img_tok), 1)
    put = (rr == ii + own_start[:, :img_tok]).astype(F32).astype(BF16)
    rb = lax.broadcasted_iota(jnp.int32, (rows, block), 0)
    here = (rb >= own_start) & (rb < own_start + img_tok) & (own_count > 0)
    for j in range(RING):
        image = dot(skip[...], down2[:, j * block:(j + 1) * block]).astype(BF16)
        moved = dot(put, image)
        old = hid[:, j * block:(j + 1) * block].astype(F32)
        xs[k, c * RING + j] = jnp.where(here, moved, old).astype(BF16)

    own = pl.ds(c * RING, RING)
    low, high = pl.ds(0, rows // 2), pl.ds(rows // 2, rows // 2)

    def x0_copy(n):
        if n == 0:
            what, peer = xs.at[k, own, low], me.at(dx=1)
        elif n == 1:
            what, peer = xs.at[k, own, high], me.at(dx=3)
        elif n == 2:
            what, peer = xs.at[k, own], side
        elif n == 5:
            what, peer = xs.at[1 - k, own, low], side
        else:
            what, peer = xs.at[1 - k, own, high], side
        return remote(what, what, sx.at[n], rx.at[n], peer)

    refs = [w_q.at[0, :, :, :, waves[0]], w_q.at[0, :, :, :, waves[1]], w_o0, w_q.at[1], w_o1]
    q0a, q0b, o0, q1, o1 = [Spread(me, ref, s1.at[i], r1.at[i], s2.at[i], r2.at[i])
                            for i, ref in enumerate(refs)]

    def landed(ref, sem):
        pltpu.make_async_copy(ref, ref, sem).wait()

    def mask_of(m):
        segment, start, count = metas[m, 0:1, :], metas[m, 1:2, :], metas[m, 2:3, :]
        one_hot = (lax.broadcasted_iota(jnp.int32, (8, rows), 0) == segment).astype(F32).astype(BF16)
        same = outer(one_hot, one_hot)
        i = lax.broadcasted_iota(jnp.int32, (rows, rows), 0)
        j = lax.broadcasted_iota(jnp.int32, (rows, rows), 1)
        in_i = (i >= start) & (i < start + img_tok) & (count > 0)
        in_j = (j >= start) & (j < start + img_tok)
        ok = (same > 0.5) & ((j <= i) | (in_i & in_j))
        bias[m] = jnp.where(ok, 0.0, -1e30)

    for w, spread in enumerate((q0a, q0b)):
        for kk in (0, 1):
            landed(w_q.at[0, z, y, kk, waves[w]], r0q.at[w, kk])
        spread.own1()
    for n in (0, 1, 2):
        x0_copy(n).start()
    section_zero(start_o)
    section_one(start_w)
    q0a.pass1()
    q0b.pass1()
    q0a.own2()
    q0b.own2()
    m_cp.wait_recv()
    g_cp.wait_recv()
    mask_of(0)
    mask_of(1)
    x0_copy(0).wait_recv()
    x0_copy(5).start()
    x0_copy(1).wait_recv()
    x0_copy(6).start()

    q0a.pass2()
    q0b.pass2()
    for kk in (0, 1):
        landed(w_o0.at[z, y, kk], r0o.at[kk])
    o0.own1()
    for n in (2, 5, 6):
        x0_copy(n).wait_recv()

    def band(m, step, first=False):
        pieces, squares = [], 0.0
        zz, yy = lax.rem(z + step, RING), lax.rem(y + step, RING)

        def take(b, at):
            values = xs[m, b, :, at].astype(F32)
            pieces.append((values * gains[0, b, :, at]).astype(BF16))
            return jnp.sum(values * values, axis=1, keepdims=True)

        half = block // 2
        depth = half // 2
        for b in (0, 1):
            for at in (0, half):
                squares += take(2 * zz + b, slice(at, at + depth))
        for b in range(RING):
            at = pl.ds(pl.multiple_of(lax.rem(yy, 2) * half + depth, depth), depth)
            squares += take(2 * b + lax.div(yy, 2), at)
        weights = jnp.concatenate(
            [w_q[0, zz, :, 0].reshape(block, acc.shape[2]), w_q[0, :, yy, 1].reshape(block, acc.shape[2])], axis=0)
        total = dot(jnp.concatenate(pieces, axis=1), weights)
        if first:
            acc[m] = total
            ssq[m] = squares
        else:
            acc[m] += total
            ssq[m] += squares

    def scaled(m):
        scale = lax.rsqrt(ssq[m] * (1.0 / (2 * RING * block)) + EPSILON)
        qkv[m] = (acc[m] * scale).astype(BF16)

    halves = [pl.ds(r * rows // 2, rows // 2) for r in (0, 1)]

    def project1(m, r):
        at = halves[r]
        squares, total = 0.0, 0.0
        for b in range(0, 2 * RING, 2):
            pieces = []
            for n in (b, b + 1):
                values = xs[m, n, at].astype(F32)
                squares += jnp.sum(values * values, axis=1, keepdims=True)
                pieces.append((values * gains[1, n]).astype(BF16))
            total += dot(jnp.concatenate(pieces, axis=1), w_q[1, b // 2].reshape(2 * block, acc.shape[2]))
        scale = lax.rsqrt(squares * (1.0 / (2 * RING * block)) + EPSILON)
        qkv[m, at] = (total * scale).astype(BF16)

    hdim = 128
    per = heads.shape[3] // hdim
    q_rows = 128

    def attend(m, r):
        for i in range(r * rows // (2 * q_rows), (r + 1) * rows // (2 * q_rows)):
            at = pl.ds(i * q_rows, q_rows)
            for h in range(per):
                base = 3 * h * hdim
                query = qkv[m, at, base:base + hdim]
                keys = qkv[m, :, base + hdim:base + 2 * hdim]
                vals = qkv[m, :, base + 2 * hdim:base + 3 * hdim]
                scores = lax.dot_general(query, keys, (((1,), (1,)), ((), ())), preferred_element_type=F32)
                scores = scores * (1.0 / math.sqrt(hdim)) + bias[m, at, :]
                probs = jnp.exp(scores - jnp.max(scores, axis=1, keepdims=True))
                probs = (probs * (1.0 / jnp.sum(probs, axis=1, keepdims=True))).astype(BF16)
                heads[m, mine, at, h * hdim:(h + 1) * hdim] = dot(probs, vals).astype(BF16)

    units = [(m, r) for m in (0, 1) for r in (0, 1)]
    h0, h1 = [[Ring(me, heads.at[m, :, halves[r]], ring_s.at[n, m, r], ring_r.at[n, m, r]) for m, r in units]
              for n in (0, 1)]
    xr = [Ring(me, xs.at[m, :, halves[r]], ring_s.at[2, m, r], ring_r.at[2, m, r]) for m, r in units]

    def mix0(m, r):
        at = halves[r]
        together = jnp.concatenate([heads[m, b, at] for b in range(2 * RING)], axis=1)
        added = dot(together, w_o0[...].reshape(2 * RING * per * hdim, block))
        xs[m, mine, at] = (xs[m, mine, at].astype(F32) + added).astype(BF16)

    def mixed(u):
        h0[u].finish()
        mix0(*units[u])
        h0[u].drain()
        xr[u].start()

    def attended(ring, u):
        attend(*units[u])
        ring[u].start()

    o0.pass1()
    for step in (0, 1, 3):
        for m in (0, 1):
            band(m, step, step == 0)
    for n in (0, 1, 2, 5, 6):
        x0_copy(n).wait_send()
    q0a.done()
    q0b.done()
    o0.own2()
    for kk in (0, 1):
        landed(w_q.at[1, z, y, kk, waves[0]], r0q.at[0, 2 + kk])
        landed(w_q.at[1, z, y, kk, waves[1]], r0q.at[1, 2 + kk])
    q1.own1()
    band(0, 2)
    scaled(0)
    attended(h0, 0)
    attended(h0, 1)

    @section_one
    def _():
        for kk in (0, 1):
            landed(w_o1.at[z, y, kk], r0w.at[kk])
        o1.own1()

    band(1, 2)
    scaled(1)
    h0[0].direct()
    attended(h0, 2)
    q1.pass1()
    o0.pass2()
    h0[0].far()
    h0[1].direct()
    attended(h0, 3)
    q1.own2()
    section_one(o1.pass1)
    o0.done()
    mixed(0)
    h0[1].far()
    h0[2].direct()
    mixed(1)
    h0[2].far()
    h0[3].direct()
    mixed(2)
    xr[0].direct()
    h0[3].far()
    mixed(3)
    q1.pass2()
    section_one(o1.own2)
    xr[0].far()
    xr[1].direct()
    xr[0].finish()
    q1.done()
    project1(0, 0)
    xr[1].far()
    xr[2].direct()
    xr[1].finish()
    project1(0, 1)
    attended(h1, 0)
    xr[2].far()
    xr[3].direct()
    attended(h1, 1)
    section_one(o1.pass2)
    xr[2].finish()
    project1(1, 0)
    xr[3].far()
    h1[0].direct()
    xr[3].finish()
    project1(1, 1)
    h1[0].far()
    h1[1].direct()
    attended(h1, 2)
    h1[1].far()
    attended(h1, 3)

    @section_zero
    def _():
        for j in range(RING):
            hid[:, j * block:(j + 1) * block] = xs[k, c * RING + j]

    h1[2].direct()
    h1[2].far()
    h1[3].direct()

    def mix1(r):
        at = halves[r]
        together = jnp.concatenate([heads[k, b, at] for b in range(2 * RING)], axis=1)
        for j in range(RING):
            cols = slice(j * block, (j + 1) * block)
            added = dot(together, w_o1[:, :, :, :, cols].reshape(2 * RING * per * hdim, block))
            hid[at, cols] = (xs[k, c * RING + j, at].astype(F32) + added).astype(BF16)

    for u in (0, 1, 2):
        h1[u].finish()

    @section_one
    def _():
        o1.done()
        mix1(0)

    h1[3].far()
    h1[3].finish()

    def tail_copy(n):
        if n == 0:
            return remote(part, got, st.at[0], rt.at[0], side)
        if n < 8:
            return remote(ys.at[place], ys.at[place], st.at[n], rt.at[n], plane(n))
        return remote(zs.at[z], zs.at[z], st.at[n], rt.at[n], me.at(dz=n - 7))

    def result_copy(n, core):
        src, dst = ((p_own, p_in), (g_own, g_in))[n]
        peer = side if core is None else dict(me.at(dx=2), tp=core)
        index = 0 if core is None else core
        return remote(src, dst, st.at[11 + 2 * n + index], rt.at[11 + n], peer)

    def send_result(n):
        @pl.when(c == 0)
        def _():
            result_copy(n, 0).start()
            result_copy(n, 1).start()

        @pl.when(c == 1)
        def _():
            result_copy(n, None).start()

    @section_one
    def _():
        @pl.when(c == 0)
        def _():
            give(7).wait_recv()
            give(8).wait_recv()

        mix1(1)
        ri = lax.broadcasted_iota(jnp.int32, (img_tok, rows), 0)
        ci = lax.broadcasted_iota(jnp.int32, (img_tok, rows), 1)
        take = (ci == ri + metas[k, 1:2, :]).astype(F32).astype(BF16)
        total = jnp.zeros(got.shape, F32)
        for j in range(RING):
            at = slice(j * block, (j + 1) * block)
            total = total + dot(dot(take, hid[:, at]).astype(BF16), up1[at, :])
        part[...] = total.astype(BF16)
        tail_copy(0).start()
        tail_copy(0).wait_recv()
        value = total + got[...].astype(F32) + skip[...].astype(F32)
        upper[...] = (value / (1.0 + jnp.exp(-value))).astype(BF16)
        present = metas[k, 2:3, :img_tok] > 0
        weighted = jnp.where(present, cots[...].astype(F32), 0.0).astype(BF16)
        ys[place] = dot(weighted, upper[...])
        for n in range(1, 8):
            tail_copy(n).start()
        guess = lax.dot_general(ups[...], upper[...], (((1,), (1,)), ((), ())), preferred_element_type=F32)
        p_own[...] = jnp.where(present, guess, 0.0).astype(BF16)
        send_result(0)
        for n in range(1, 8):
            tail_copy(n).wait()
        in_plane = ys[0]
        for n in range(1, 8):
            in_plane = in_plane + ys[n]
        zs[z] = in_plane
        for n in (8, 9, 10):
            tail_copy(n).start()
        for n in (8, 9, 10):
            tail_copy(n).wait()
        g_own[...] = zs[0] + zs[1] + zs[2] + zs[3]
        send_result(1)
        tail_copy(0).wait_send()

    for j in (1, 2, 3):
        for w in (0, 1):
            scatter_q(j, w).wait_send()

    @section_zero
    def _():
        for j in (1, 2, 3):
            scatter_o(j).wait_send()

        @pl.when(c == 0)
        def _():
            give(7).wait_send()
            give(8).wait_send()

    @section_one
    def _():
        whole_o().wait_send()
        o1.drain()

    g_cp.wait_send()
    m_cp.wait_send()
    for g in (q0a, q0b, o0, q1):
        g.drain()
    for r in h1 + xr:
        r.drain()

    @pl.when((s == 1) & (c == 1))
    def _():
        pred[...] = p_own[...]
        grad[...] = g_own[...]
        result_copy(0, None).wait_send()
        result_copy(1, None).wait_send()

    @pl.when((s == 0) | (c == 0))
    def _():
        result_copy(0, None).wait_recv()
        result_copy(1, None).wait_recv()
        pred[...] = p_in[...]
        grad[...] = g_in[...]

    @pl.when((s == 1) & (c == 0))
    def _():
        for n in (0, 1):
            for core in (0, 1):
                result_copy(n, core).wait_send()


def window(wq, wo, tokens, patches_t, wd1, wd2, wu1, wu2_t, gain, segment, start, count, cot_t):
    rows, width = tokens.shape
    block = width // RING
    depth, wide_q = wq.shape[1:]
    depth_o = wo.shape[0]
    img_tok = patches_t.shape[1]
    channels = wd1.shape[1]
    pix = wu2_t.shape[0]
    head_cols = wide_q // 3
    dma = pltpu.SemaphoreType.DMA
    vm = pltpu.VMEM
    scratch = [
        vm((2, RING, RING, 2, depth, wide_q), BF16),
        vm((RING, RING, 2, depth_o, block), BF16),
        vm((RING, RING, 2, depth_o, width), BF16),
        vm((2, 2 * RING, rows, block), BF16),
        vm((2, 2 * RING, rows, head_cols), BF16),
        vm((2, rows, wide_q), F32),
        vm((2, rows, wide_q), BF16),
        vm((2, rows, rows), F32),
        vm((2, rows, 1), F32),
        vm((2,) + gain.shape, F32),
        vm((2, 8, rows), jnp.int32),
        vm((img_tok, channels), BF16),
        vm(wd2.shape, BF16),
        vm(wu1.shape, BF16),
        vm((img_tok, channels), BF16),
        vm((img_tok, channels), BF16),
        vm((img_tok, channels), BF16),
        vm(cot_t.shape, BF16),
        vm(wu2_t.shape, BF16),
        vm((pix, img_tok), BF16),
        vm((pix, img_tok), BF16),
        vm((pix, channels), F32),
        vm((pix, channels), F32),
        vm((2 * RING, pix, channels), F32),
        vm((RING, pix, channels), F32),
        dma((2, 4)), dma((2, 4)), dma((4,)), dma((2,)), dma((1,)), dma((2,)),
        dma((5, 2, 4)), dma((5, 2, 4)), dma((5, 2, 4)), dma((5, 2, 4)),
        dma((3, 2, 2, 8)), dma((3, 2, 2, 8)), dma((9,)), dma((9,)), dma((15,)), dma((13,)), dma((4,)),
    ]
    sm = pl.BlockSpec(memory_space=pltpu.SMEM)
    return pl.pallas_call(
        kernel,
        out_shape=(
            jax.ShapeDtypeStruct((rows, width), BF16),
            jax.ShapeDtypeStruct((pix, img_tok), BF16),
            jax.ShapeDtypeStruct((pix, channels), F32),
        ),
        in_specs=[ANY, ANY, ANY, VM, VM, ANY, ANY, VM, ANY, VM, sm, sm, VM],
        out_specs=(VM, VM, VM),
        scratch_shapes=scratch,
        compiler_params=pltpu.CompilerParams(collective_id=0, has_side_effects=True,
                                             vmem_limit_bytes=63 << 20),
        name="window",
    )(wq, wo, tokens, patches_t, wd1, wd2, wu1, wu2_t, gain, segment, start, count, cot_t)


def shards(
    tokens_in, patches, segment_ids, img_start, img_count, norm_gain, w_qkv, w_out, w_down1, w_down2,
    w_up1, w_up2, cotangent,
):
    rows, width = tokens_in.shape[1:]
    depth, heads, three, hdim = w_qkv.shape[1:]
    wide_q = heads // RING * three * hdim
    block = width // RING
    wq = jnp.transpose(w_qkv[0].reshape(depth, RING, wide_q), (1, 0, 2))
    gain = norm_gain.reshape(2 * RING, 1, block)
    hidden, pred, grad = window(wq, w_out[0], tokens_in[0], patches[0].T, w_down1, w_down2, w_up1,
                                w_up2.T, gain, segment_ids, img_start, img_count, cotangent[0].T)
    return (hidden[None, None], pred.T[None], grad.T)


def solution(mesh):
    placed = (
        P("dp", None, "tp"),
        P("dp", None, None),
        P("dp", None),
        P("dp"),
        P("dp"),
        P("section", None),
        P("section", "dp", "tp", None, None),
        P("section", "dp", "tp"),
        P(),
        P(None, "tp"),
        P("tp", None),
        P(None, "section"),
        P("dp", None, "section"),
    )
    return jax.shard_map(
        shards,
        mesh=mesh,
        in_specs=placed,
        out_specs=(P("section", "dp", None, "tp"), P("dp", None, "section"), P(None, "section")),
        check_vma=False,
    )
```

```python
import math

import jax
import jax.numpy as jnp
from jax import lax
from jax.experimental import pallas as pl
from jax.experimental.pallas import tpu as pltpu
from jax.sharding import PartitionSpec as P

EPSILON = 1e-05
MESH = pl.DeviceIdType.MESH
ANY = pl.BlockSpec(memory_space=pl.ANY)
VM = pl.BlockSpec(memory_space=pltpu.VMEM)
RING = 4
BF16, F32 = jnp.bfloat16, jnp.float32


def dot(a, b):
    return jnp.dot(a, b, preferred_element_type=F32)


def outer(a, b):
    return lax.dot_general(a, b, (((0,), (0,)), ((), ())), preferred_element_type=F32)


class Place:
    def __init__(self):
        self.s = lax.axis_index("section")
        self.c = lax.axis_index("tp")
        d = lax.axis_index("dp")
        self.k = lax.rem(d, 2)
        self.y = lax.rem(lax.div(d, 2), RING)
        self.z = lax.div(d, 2 * RING)
        self.x = 2 * self.s + self.k

    def at(self, dx=0, dy=0, dz=0, sibling=False):
        x = lax.rem(self.x + dx, RING)
        y = lax.rem(self.y + dy, RING)
        z = lax.rem(self.z + dz, RING)
        return {
            "section": lax.div(x, 2),
            "tp": 1 - self.c if sibling else self.c,
            "dp": z * 8 + y * 2 + lax.rem(x, 2),
        }

    def partner(self):
        return {"section": self.s, "tp": self.c, "dp": self.z * 8 + self.y * 2 + 1 - self.k}


def remote(src, dst, send, recv, peer):
    return pltpu.make_async_remote_copy(
        src_ref=src, dst_ref=dst, send_sem=send, recv_sem=recv, device_id=peer, device_id_type=MESH
    )


class Spread:
    def __init__(self, me, ref, s1, r1, s2, r2):
        self.me, self.ref, self.sems = me, ref, (s1, r1, s2, r2)

    def first(self, kk, n):
        me, ref = self.me, self.ref
        s1, r1 = self.sems[:2]
        step = 1 if n % 2 == 0 else 3
        peer = me.at(dy=step) if kk == 0 else me.at(dz=step)
        if n < 2:
            part = ref.at[me.z, me.y, kk]
        else:
            back = 4 - step
            zz = me.z if kk == 0 else lax.rem(me.z + back, RING)
            yy = lax.rem(me.y + back, RING) if kk == 0 else me.y
            half = ref.shape[3] // 2
            part = ref.at[zz, yy, kk, pl.ds((n - 2) * half, half)]
        return remote(part, part, s1.at[kk, n], r1.at[kk, n], peer)

    def second(self, kk, n):
        me, ref = self.me, self.ref
        s2, r2 = self.sems[2:]
        step = 1 if n % 2 == 0 else 3
        peer = me.at(dz=step) if kk == 0 else me.at(dy=step)
        if n < 2:
            part = ref.at[me.z, :, kk] if kk == 0 else ref.at[:, me.y, kk]
        else:
            piece = pl.ds(2 * (n - 2), 2)
            back = 4 - step
            if kk == 0:
                part = ref.at[lax.rem(me.z + back, RING), piece, kk]
            else:
                part = ref.at[piece, lax.rem(me.y + back, RING), kk]
        return remote(part, part, s2.at[kk, n], r2.at[kk, n], peer)

    def own1(self):
        for kk in (0, 1):
            for n in (0, 1):
                self.first(kk, n).start()

    def pass1(self):
        for kk in (0, 1):
            for n in (0, 1):
                self.first(kk, n).wait_recv()
                self.first(kk, n + 2).start()

    def own2(self):
        for kk in (0, 1):
            for n in (2, 3):
                self.first(kk, n).wait_recv()
            for n in (0, 1):
                self.second(kk, n).start()

    def pass2(self):
        for kk in (0, 1):
            for n in (0, 1):
                self.second(kk, n).wait_recv()
                self.second(kk, n + 2).start()

    def done(self):
        for kk in (0, 1):
            for n in (2, 3):
                self.second(kk, n).wait_recv()

    def drain(self):
        for kk in (0, 1):
            for n in range(4):
                self.first(kk, n).wait_send()
                self.second(kk, n).wait_send()


class Ring:
    def __init__(self, me, ref, ss, rs):
        self.me, self.ref, self.ss, self.rs = me, ref, ss, rs

    def copy(self, n):
        me, ref = self.me, self.ref
        half = ref.shape[1] // 2

        def block(back):
            return me.c * RING + lax.rem(me.x + back, RING)

        up, down, side = me.at(dx=1), me.at(dx=3), me.at(sibling=True)
        part, peer = (
            lambda: (ref.at[block(0)], up),
            lambda: (ref.at[block(0)], down),
            lambda: (ref.at[block(0)], side),
            lambda: (ref.at[block(3), pl.ds(0, half)], up),
            lambda: (ref.at[block(1), pl.ds(half, half)], down),
            lambda: (ref.at[block(3)], side),
            lambda: (ref.at[block(1)], side),
            lambda: (ref.at[block(2)], side),
        )[n]()
        return remote(part, part, self.ss.at[n], self.rs.at[n], peer)

    def start(self):
        for n in (0, 1, 2):
            self.copy(n).start()

    def direct(self):
        self.copy(0).wait_recv()
        self.copy(3).start()
        self.copy(5).start()
        self.copy(1).wait_recv()
        self.copy(4).start()
        self.copy(6).start()

    def far(self):
        self.copy(3).wait_recv()
        self.copy(4).wait_recv()
        self.copy(7).start()

    def finish(self):
        for n in (2, 5, 6, 7):
            self.copy(n).wait_recv()

    def drain(self):
        for n in range(8):
            self.copy(n).wait_send()


def kernel(
    wq, wo, tokens, patches_t, wd1, wd2, wu1, wu2_t, gain, segment, start_in, count_in, cot_t,
    hid, pred, grad,
    w_q, w_o0, w_o1, xs, heads, acc, qkv, bias, ssq, gains, metas, skip, down2, up1,
    part, got, upper, cots, ups, p_own, p_in, g_own, g_in, ys, zs,
    s0q, r0q, s0o, r0o, s0w, r0w, s1, r1, s2, r2, ring_s, ring_r, sx, rx, st, rt, loc,
):
    me = Place()
    s, c, k, x, y, z = me.s, me.c, me.k, me.x, me.y, me.z
    rows = tokens.shape[0]
    img_tok = patches_t.shape[1]
    block = xs.shape[3]
    mine = c * RING + x
    side = me.at(sibling=True)

    loads = [
        pltpu.make_async_copy(tokens, hid, loc.at[0]),
        pltpu.make_async_copy(wd2, down2, loc.at[1]),
        pltpu.make_async_copy(wu1, up1, loc.at[2]),
        pltpu.make_async_copy(gain, gains.at[s], loc.at[3]),
    ]
    for cp in loads:
        cp.start()
    metas[k, 0:1, :] = segment[...]
    metas[k, 1:2, :] = jnp.full((1, rows), start_in[0], jnp.int32)
    metas[k, 2:3, :] = jnp.full((1, rows), count_in[0], jnp.int32)
    metas[k, 3:8, :] = jnp.zeros((5, rows), jnp.int32)

    place = 2 * y + k

    def plane(n):
        return {"section": s, "tp": c, "dp": 8 * z + lax.rem(place + n, 8)}

    peers = ([me.at(dx=j) for j in (1, 2, 3)] + [plane(n) for n in range(1, 8)]
             + [me.at(dz=j) for j in (1, 2, 3)] + [side])
    across = dict(me.at(dx=2), tp=1 - c)
    barrier = pltpu.get_barrier_semaphore()
    for peer in peers + [across]:
        pl.semaphore_signal(barrier, inc=1, device_id=peer, device_id_type=MESH)
    pl.semaphore_wait(barrier, len(peers) + 1)

    depth = wq.shape[1]
    waves = [pl.ds(w * depth // 2, depth // 2) for w in (0, 1)]

    def scatter_q(j, w):
        return remote(wq.at[lax.rem(x + j, RING), waves[w]], w_q.at[s, z, y, k, waves[w]], s0q.at[w, j],
                      r0q.at[w, x], me.at(dx=j))

    def scatter_o(j):
        cols = pl.ds(pl.multiple_of(lax.rem(x + j, RING) * block, block), block)
        return remote(wo.at[:, cols], w_o0.at[z, y, k], s0o.at[j], r0o.at[k], me.at(dx=j))

    def whole_o():
        return remote(wo, w_o1.at[z, y, k], s0w.at[0], r0w.at[k], me.partner())

    def start_q():
        for w in (0, 1):
            for j in (1, 3, 2):
                scatter_q(j, w).start()
            pltpu.make_async_copy(wq.at[x, waves[w]], w_q.at[s, z, y, k, waves[w]], r0q.at[w, x]).start()

    def start_o():
        for j in (1, 3, 2):
            scatter_o(j).start()
        own_cols = pl.ds(pl.multiple_of(x * block, block), block)
        pltpu.make_async_copy(wo.at[:, own_cols], w_o0.at[z, y, k], r0o.at[k]).start()

    def start_w():
        whole_o().start()
        pltpu.make_async_copy(wo, w_o1.at[z, y, k], r0w.at[k]).start()

    section_zero, section_one = pl.when(s == 0), pl.when(s == 1)
    start_q()

    for cp in loads:
        cp.wait()
    g_cp = remote(gains.at[s], gains.at[s], sx.at[3], rx.at[3], me.at(dx=2))
    m_cp = remote(metas.at[k], metas.at[k], sx.at[4], rx.at[4], me.at(dx=1))
    g_cp.start()
    m_cp.start()

    def give(n):
        src, dst = ((cot_t, cots), (wu2_t, ups))[n - 7]
        return remote(src, dst, sx.at[n], rx.at[n], me.at(dx=2))

    @pl.when((s == 0) & (c == 0))
    def _():
        give(7).start()
        give(8).start()

    @pl.when((s == 1) & (c == 1))
    def _():
        cots[...] = cot_t[...]
        ups[...] = wu2_t[...]

    inner = outer(patches_t[...], wd1[...])
    skip[...] = (inner / (1.0 + jnp.exp(-inner))).astype(BF16)
    own_start, own_count = metas[k, 1:2, :], metas[k, 2:3, :]
    rr = lax.broadcasted_iota(jnp.int32, (rows, img_tok), 0)
    ii = lax.broadcasted_iota(jnp.int32, (rows, img_tok), 1)
    put = (rr == ii + own_start[:, :img_tok]).astype(F32).astype(BF16)
    rb = lax.broadcasted_iota(jnp.int32, (rows, block), 0)
    here = (rb >= own_start) & (rb < own_start + img_tok) & (own_count > 0)
    for j in range(RING):
        image = dot(skip[...], down2[:, j * block:(j + 1) * block]).astype(BF16)
        moved = dot(put, image)
        old = hid[:, j * block:(j + 1) * block].astype(F32)
        xs[k, c * RING + j] = jnp.where(here, moved, old).astype(BF16)

    own = pl.ds(c * RING, RING)
    low, high = pl.ds(0, rows // 2), pl.ds(rows // 2, rows // 2)

    def x0_copy(n):
        if n == 0:
            what, peer = xs.at[k, own, low], me.at(dx=1)
        elif n == 1:
            what, peer = xs.at[k, own, high], me.at(dx=3)
        elif n == 2:
            what, peer = xs.at[k, own], side
        elif n == 5:
            what, peer = xs.at[1 - k, own, low], side
        else:
            what, peer = xs.at[1 - k, own, high], side
        return remote(what, what, sx.at[n], rx.at[n], peer)

    refs = [w_q.at[0, :, :, :, waves[0]], w_q.at[0, :, :, :, waves[1]], w_o0, w_q.at[1], w_o1]
    q0a, q0b, o0, q1, o1 = [Spread(me, ref, s1.at[i], r1.at[i], s2.at[i], r2.at[i])
                            for i, ref in enumerate(refs)]

    def landed(ref, sem):
        pltpu.make_async_copy(ref, ref, sem).wait()

    def mask_of(m):
        segment, start, count = metas[m, 0:1, :], metas[m, 1:2, :], metas[m, 2:3, :]
        one_hot = (lax.broadcasted_iota(jnp.int32, (8, rows), 0) == segment).astype(F32).astype(BF16)
        same = outer(one_hot, one_hot)
        i = lax.broadcasted_iota(jnp.int32, (rows, rows), 0)
        j = lax.broadcasted_iota(jnp.int32, (rows, rows), 1)
        in_i = (i >= start) & (i < start + img_tok) & (count > 0)
        in_j = (j >= start) & (j < start + img_tok)
        ok = (same > 0.5) & ((j <= i) | (in_i & in_j))
        bias[m] = jnp.where(ok, 0.0, -1e30)

    for w, spread in enumerate((q0a, q0b)):
        for kk in (0, 1):
            landed(w_q.at[0, z, y, kk, waves[w]], r0q.at[w, kk])
        spread.own1()
    for n in (0, 1, 2):
        x0_copy(n).start()
    section_zero(start_o)
    section_one(start_w)
    q0a.pass1()
    q0b.pass1()
    q0a.own2()
    q0b.own2()
    m_cp.wait_recv()
    g_cp.wait_recv()
    mask_of(0)
    mask_of(1)
    x0_copy(0).wait_recv()
    x0_copy(5).start()
    x0_copy(1).wait_recv()
    x0_copy(6).start()

    q0a.pass2()
    q0b.pass2()
    for kk in (0, 1):
        landed(w_o0.at[z, y, kk], r0o.at[kk])
    o0.own1()
    for n in (2, 5, 6):
        x0_copy(n).wait_recv()

    def band(m, step, first=False):
        pieces, squares = [], 0.0
        zz, yy = lax.rem(z + step, RING), lax.rem(y + step, RING)

        def take(b, at):
            values = xs[m, b, :, at].astype(F32)
            pieces.append((values * gains[0, b, :, at]).astype(BF16))
            return jnp.sum(values * values, axis=1, keepdims=True)

        half = block // 2
        depth = half // 2
        for b in (0, 1):
            for at in (0, half):
                squares += take(2 * zz + b, slice(at, at + depth))
        for b in range(RING):
            at = pl.ds(pl.multiple_of(lax.rem(yy, 2) * half + depth, depth), depth)
            squares += take(2 * b + lax.div(yy, 2), at)
        weights = jnp.concatenate(
            [w_q[0, zz, :, 0].reshape(block, acc.shape[2]), w_q[0, :, yy, 1].reshape(block, acc.shape[2])], axis=0)
        total = dot(jnp.concatenate(pieces, axis=1), weights)
        if first:
            acc[m] = total
            ssq[m] = squares
        else:
            acc[m] += total
            ssq[m] += squares

    def scaled(m):
        scale = lax.rsqrt(ssq[m] * (1.0 / (2 * RING * block)) + EPSILON)
        qkv[m] = (acc[m] * scale).astype(BF16)

    halves = [pl.ds(r * rows // 2, rows // 2) for r in (0, 1)]

    def project1(m, r):
        at = halves[r]
        squares, total = 0.0, 0.0
        for b in range(0, 2 * RING, 2):
            pieces = []
            for n in (b, b + 1):
                values = xs[m, n, at].astype(F32)
                squares += jnp.sum(values * values, axis=1, keepdims=True)
                pieces.append((values * gains[1, n]).astype(BF16))
            total += dot(jnp.concatenate(pieces, axis=1), w_q[1, b // 2].reshape(2 * block, acc.shape[2]))
        scale = lax.rsqrt(squares * (1.0 / (2 * RING * block)) + EPSILON)
        qkv[m, at] = (total * scale).astype(BF16)

    hdim = 128
    per = heads.shape[3] // hdim
    q_rows = 128

    def attend(m, r):
        for i in range(r * rows // (2 * q_rows), (r + 1) * rows // (2 * q_rows)):
            at = pl.ds(i * q_rows, q_rows)
            for h in range(per):
                base = 3 * h * hdim
                query = qkv[m, at, base:base + hdim]
                keys = qkv[m, :, base + hdim:base + 2 * hdim]
                vals = qkv[m, :, base + 2 * hdim:base + 3 * hdim]
                scores = lax.dot_general(query, keys, (((1,), (1,)), ((), ())), preferred_element_type=F32)
                scores = scores * (1.0 / math.sqrt(hdim)) + bias[m, at, :]
                probs = jnp.exp(scores - jnp.max(scores, axis=1, keepdims=True))
                probs = (probs * (1.0 / jnp.sum(probs, axis=1, keepdims=True))).astype(BF16)
                heads[m, mine, at, h * hdim:(h + 1) * hdim] = dot(probs, vals).astype(BF16)

    units = [(m, r) for m in (0, 1) for r in (0, 1)]
    h0, h1 = [[Ring(me, heads.at[m, :, halves[r]], ring_s.at[n, m, r], ring_r.at[n, m, r]) for m, r in units]
              for n in (0, 1)]
    xr = [Ring(me, xs.at[m, :, halves[r]], ring_s.at[2, m, r], ring_r.at[2, m, r]) for m, r in units]

    def mix0(m, r):
        at = halves[r]
        together = jnp.concatenate([heads[m, b, at] for b in range(2 * RING)], axis=1)
        added = dot(together, w_o0[...].reshape(2 * RING * per * hdim, block))
        xs[m, mine, at] = (xs[m, mine, at].astype(F32) + added).astype(BF16)

    def mixed(u):
        h0[u].finish()
        mix0(*units[u])
        h0[u].drain()
        xr[u].start()

    def attended(ring, u):
        attend(*units[u])
        ring[u].start()

    o0.pass1()
    for step in (0, 1, 3):
        for m in (0, 1):
            band(m, step, step == 0)
    for n in (0, 1, 2, 5, 6):
        x0_copy(n).wait_send()
    q0a.done()
    q0b.done()
    o0.own2()
    for kk in (0, 1):
        landed(w_q.at[1, z, y, kk, waves[0]], r0q.at[0, 2 + kk])
        landed(w_q.at[1, z, y, kk, waves[1]], r0q.at[1, 2 + kk])
    q1.own1()
    band(0, 2)
    scaled(0)
    attended(h0, 0)
    attended(h0, 1)

    @section_one
    def _():
        for kk in (0, 1):
            landed(w_o1.at[z, y, kk], r0w.at[kk])
        o1.own1()

    band(1, 2)
    scaled(1)
    h0[0].direct()
    attended(h0, 2)
    q1.pass1()
    o0.pass2()
    h0[0].far()
    h0[1].direct()
    attended(h0, 3)
    q1.own2()
    section_one(o1.pass1)
    o0.done()
    mixed(0)
    h0[1].far()
    h0[2].direct()
    mixed(1)
    h0[2].far()
    h0[3].direct()
    mixed(2)
    xr[0].direct()
    h0[3].far()
    mixed(3)
    q1.pass2()
    xr[0].far()
    xr[1].direct()
    xr[0].finish()
    q1.done()
    section_one(o1.own2)
    project1(0, 0)
    xr[1].far()
    xr[2].direct()
    xr[1].finish()
    project1(0, 1)
    attended(h1, 0)
    xr[2].far()
    xr[3].direct()
    attended(h1, 1)
    xr[2].finish()
    project1(1, 0)
    section_one(o1.pass2)
    xr[3].far()
    h1[0].direct()
    xr[3].finish()
    project1(1, 1)
    h1[0].far()
    h1[1].direct()
    attended(h1, 2)
    h1[1].far()
    attended(h1, 3)

    h1[2].direct()
    h1[2].far()
    h1[3].direct()

    def mix1(r):
        at = halves[r]
        together = jnp.concatenate([heads[k, b, at] for b in range(2 * RING)], axis=1)
        for j in range(RING):
            cols = slice(j * block, (j + 1) * block)
            added = dot(together, w_o1[:, :, :, :, cols].reshape(2 * RING * per * hdim, block))
            hid[at, cols] = (xs[k, c * RING + j, at].astype(F32) + added).astype(BF16)

    for u in (0, 1, 2):
        h1[u].finish()

    @section_one
    def _():
        o1.done()
        mix1(0)

    h1[3].far()
    h1[3].finish()

    @section_zero
    def _():
        for j in range(RING):
            hid[:, j * block:(j + 1) * block] = xs[k, c * RING + j]

    def tail_copy(n):
        if n == 0:
            return remote(part, got, st.at[0], rt.at[0], side)
        if n < 8:
            return remote(ys.at[place], ys.at[place], st.at[n], rt.at[n], plane(n))
        return remote(zs.at[z], zs.at[z], st.at[n], rt.at[n], me.at(dz=n - 7))

    def result_copy(n, core):
        src, dst = ((p_own, p_in), (g_own, g_in))[n]
        peer = side if core is None else dict(me.at(dx=2), tp=core)
        index = 0 if core is None else core
        return remote(src, dst, st.at[11 + 2 * n + index], rt.at[11 + n], peer)

    def send_result(n):
        @pl.when(c == 0)
        def _():
            result_copy(n, 0).start()
            result_copy(n, 1).start()

        @pl.when(c == 1)
        def _():
            result_copy(n, None).start()

    @section_one
    def _():
        @pl.when(c == 0)
        def _():
            give(7).wait_recv()
            give(8).wait_recv()

        mix1(1)
        ri = lax.broadcasted_iota(jnp.int32, (img_tok, rows), 0)
        ci = lax.broadcasted_iota(jnp.int32, (img_tok, rows), 1)
        take = (ci == ri + metas[k, 1:2, :]).astype(F32).astype(BF16)
        total = jnp.zeros(got.shape, F32)
        for j in range(RING):
            at = slice(j * block, (j + 1) * block)
            total = total + dot(dot(take, hid[:, at]).astype(BF16), up1[at, :])
        part[...] = total.astype(BF16)
        tail_copy(0).start()
        tail_copy(0).wait_recv()
        value = total + got[...].astype(F32) + skip[...].astype(F32)
        upper[...] = (value / (1.0 + jnp.exp(-value))).astype(BF16)
        present = metas[k, 2:3, :img_tok] > 0
        weighted = jnp.where(present, cots[...].astype(F32), 0.0).astype(BF16)
        ys[place] = dot(weighted, upper[...])
        for n in range(1, 8):
            tail_copy(n).start()
        guess = lax.dot_general(ups[...], upper[...], (((1,), (1,)), ((), ())), preferred_element_type=F32)
        p_own[...] = jnp.where(present, guess, 0.0).astype(BF16)
        send_result(0)
        for n in range(1, 8):
            tail_copy(n).wait()
        in_plane = ys[0]
        for n in range(1, 8):
            in_plane = in_plane + ys[n]
        zs[z] = in_plane
        for n in (8, 9, 10):
            tail_copy(n).start()
        for n in (8, 9, 10):
            tail_copy(n).wait()
        g_own[...] = zs[0] + zs[1] + zs[2] + zs[3]
        send_result(1)
        tail_copy(0).wait_send()

    for j in (1, 2, 3):
        for w in (0, 1):
            scatter_q(j, w).wait_send()

    @section_zero
    def _():
        for j in (1, 2, 3):
            scatter_o(j).wait_send()

        @pl.when(c == 0)
        def _():
            give(7).wait_send()
            give(8).wait_send()

    @section_one
    def _():
        whole_o().wait_send()
        o1.drain()

    g_cp.wait_send()
    m_cp.wait_send()
    for g in (q0a, q0b, o0, q1):
        g.drain()
    for r in h1 + xr:
        r.drain()

    @pl.when((s == 1) & (c == 1))
    def _():
        pred[...] = p_own[...]
        grad[...] = g_own[...]
        result_copy(0, None).wait_send()
        result_copy(1, None).wait_send()

    @pl.when((s == 0) | (c == 0))
    def _():
        result_copy(0, None).wait_recv()
        result_copy(1, None).wait_recv()
        pred[...] = p_in[...]
        grad[...] = g_in[...]

    @pl.when((s == 1) & (c == 0))
    def _():
        for n in (0, 1):
            for core in (0, 1):
                result_copy(n, core).wait_send()


def window(wq, wo, tokens, patches_t, wd1, wd2, wu1, wu2_t, gain, segment, start, count, cot_t):
    rows, width = tokens.shape
    block = width // RING
    depth, wide_q = wq.shape[1:]
    depth_o = wo.shape[0]
    img_tok = patches_t.shape[1]
    channels = wd1.shape[1]
    pix = wu2_t.shape[0]
    head_cols = wide_q // 3
    dma = pltpu.SemaphoreType.DMA
    vm = pltpu.VMEM
    scratch = [
        vm((2, RING, RING, 2, depth, wide_q), BF16),
        vm((RING, RING, 2, depth_o, block), BF16),
        vm((RING, RING, 2, depth_o, width), BF16),
        vm((2, 2 * RING, rows, block), BF16),
        vm((2, 2 * RING, rows, head_cols), BF16),
        vm((2, rows, wide_q), F32),
        vm((2, rows, wide_q), BF16),
        vm((2, rows, rows), F32),
        vm((2, rows, 1), F32),
        vm((2,) + gain.shape, F32),
        vm((2, 8, rows), jnp.int32),
        vm((img_tok, channels), BF16),
        vm(wd2.shape, BF16),
        vm(wu1.shape, BF16),
        vm((img_tok, channels), BF16),
        vm((img_tok, channels), BF16),
        vm((img_tok, channels), BF16),
        vm(cot_t.shape, BF16),
        vm(wu2_t.shape, BF16),
        vm((pix, img_tok), BF16),
        vm((pix, img_tok), BF16),
        vm((pix, channels), F32),
        vm((pix, channels), F32),
        vm((2 * RING, pix, channels), F32),
        vm((RING, pix, channels), F32),
        dma((2, 4)), dma((2, 4)), dma((4,)), dma((2,)), dma((1,)), dma((2,)),
        dma((5, 2, 4)), dma((5, 2, 4)), dma((5, 2, 4)), dma((5, 2, 4)),
        dma((3, 2, 2, 8)), dma((3, 2, 2, 8)), dma((9,)), dma((9,)), dma((15,)), dma((13,)), dma((4,)),
    ]
    sm = pl.BlockSpec(memory_space=pltpu.SMEM)
    return pl.pallas_call(
        kernel,
        out_shape=(
            jax.ShapeDtypeStruct((rows, width), BF16),
            jax.ShapeDtypeStruct((pix, img_tok), BF16),
            jax.ShapeDtypeStruct((pix, channels), F32),
        ),
        in_specs=[ANY, ANY, ANY, VM, VM, ANY, ANY, VM, ANY, VM, sm, sm, VM],
        out_specs=(VM, VM, VM),
        scratch_shapes=scratch,
        compiler_params=pltpu.CompilerParams(collective_id=0, has_side_effects=True,
                                             vmem_limit_bytes=63 << 20),
        name="window",
    )(wq, wo, tokens, patches_t, wd1, wd2, wu1, wu2_t, gain, segment, start, count, cot_t)


def shards(
    tokens_in, patches, segment_ids, img_start, img_count, norm_gain, w_qkv, w_out, w_down1, w_down2,
    w_up1, w_up2, cotangent,
):
    rows, width = tokens_in.shape[1:]
    depth, heads, three, hdim = w_qkv.shape[1:]
    wide_q = heads // RING * three * hdim
    block = width // RING
    wq = jnp.transpose(w_qkv[0].reshape(depth, RING, wide_q), (1, 0, 2))
    gain = norm_gain.reshape(2 * RING, 1, block)
    hidden, pred, grad = window(wq, w_out[0], tokens_in[0], patches[0].T, w_down1, w_down2, w_up1,
                                w_up2.T, gain, segment_ids, img_start, img_count, cotangent[0].T)
    return (hidden[None, None], pred.T[None], grad.T)


def solution(mesh):
    placed = (
        P("dp", None, "tp"),
        P("dp", None, None),
        P("dp", None),
        P("dp"),
        P("dp"),
        P("section", None),
        P("section", "dp", "tp", None, None),
        P("section", "dp", "tp"),
        P(),
        P(None, "tp"),
        P("tp", None),
        P(None, "section"),
        P("dp", None, "section"),
    )
    return jax.shard_map(
        shards,
        mesh=mesh,
        in_specs=placed,
        out_specs=(P("section", "dp", None, "tp"), P("dp", None, "section"), P(None, "section")),
        check_vma=False,
    )
```
